32 devices in a mesh: clip: 2 (over x), frame: 8 (over z, y), band: 2 (over core).
Axes of the slice: x: 2, y: 2, z: 4, core: 2. Of those that a mesh axis runs over, the one named last changes fastest.
Arguments:
- pixels: bfloat16 [16, 16, 32, 256], P(('clip', 'frame'), 'band'), parts along dimension 0, may hold values from -40 to 40
- gru_state: bfloat16 [16, 16, 32, 128], P(('clip', 'frame'), 'band'), parts along dimension 0, may hold values from -1 to 1
- tokens: bfloat16 [16, 1024, 256], P(('clip', 'frame'), 'band'), parts along dimension 0, may hold values from -30 to 30
- visible: int32 [16, 1024], P(('clip', 'frame'), 'band'), parts along dimension 0, may hold values from 0 to 1, as said below
- query_frame: int32 [2048], P(('clip', 'band')), parts along dimension 0, may hold values from 0 to 7, as said below
- pixel_query: bfloat16 [256, 256], replicated, may hold values from -2 to 2
- pixel_key: bfloat16 [256, 256], replicated, may hold values from -2 to 2
- pixel_value: bfloat16 [256, 256], replicated, may hold values from -0.375 to 0.375
- pixel_out: bfloat16 [256, 128], replicated, may hold values from -1.5 to 1.5
- time_query: bfloat16 [256, 256], replicated, may hold values from -2 to 2
- time_key: bfloat16 [256, 256], replicated, may hold values from -2 to 2
- time_value: bfloat16 [256, 256], replicated, may hold values from -0.375 to 0.375
- time_out: bfloat16 [256, 256], replicated, may hold values from -0.75 to 0.75
- gru_gates: bfloat16 [3, 3, 256, 256], replicated, may hold values from -0.125 to 0.125
- gru_candidate: bfloat16 [3, 3, 256, 128], replicated, may hold values from -0.125 to 0.125
Outputs:
- refined_state: bfloat16 [16, 16, 32, 128], P(('clip', 'frame'), 'band'), parts along dimension 0
- track_out: bfloat16 [16, 1024, 256], P(('clip', 'frame'), 'band'), parts along dimension 0
The draws below stay inside these ranges and needn't reach their ends.
There are 2 independent parts, one for each index of `clip`. The reference program is written for one: setup_inputs(seed, part) draws one part's arguments, and reference() takes and returns one part's arrays. A program takes and returns all parts, laid end to end along the dimension named above; an argument that names none is the same for every part. Nothing has to cross between parts.
Inputs may be any that keep to these rules, and one draw needn't show every extreme that they name: Each track is visible in the frame named by its query frame index. `query_frame`: every frame is the query frame of exactly 128 tracks.
All inputs are finite; a program needn't handle non-finite values.
Results may differ from the reference program's by a relative error of at most 0.0095.
The reference program's roundings to bfloat16 on the way count: a program that leaves them out, or rounds other values in their place, can miss the bound.
Values may be sent and summed in bfloat16 or wider, within the bound.
A program may use at most 64 MiB of HBM per device.

```python
import math
import jax
import jax.numpy as jnp
from jax import lax

CHANNELS = 256
HEADS = 8
HEAD_DIM = 32
GRU_WIDTH = 128
TRACKS = 1024
WIDTH = 32
ITERS = 2
FRAMES = 8
ROWS = 16


def draw_pixels(key, part):
    full_shape = (FRAMES, ROWS, WIDTH, CHANNELS)
    drawn = jnp.clip(jax.random.normal(jax.random.fold_in(key, 502), full_shape, jnp.float32), -4.0, 4.0)
    return drawn.astype(jnp.bfloat16)


def draw_tokens(key, part):
    full_shape = (FRAMES, TRACKS, CHANNELS)
    drawn = jnp.clip(jax.random.normal(jax.random.fold_in(key, 506), full_shape, jnp.float32), -4.0, 4.0)
    return drawn.astype(jnp.bfloat16)


def track_layout(key):
    shuffled = jax.random.permutation(jax.random.fold_in(key, 701), TRACKS)
    anchor_frames = (shuffled % FRAMES).astype(jnp.int32)
    coin_flips = jax.random.randint(jax.random.fold_in(key, 702), (FRAMES, TRACKS), 0, 5)
    frame_ids = jnp.arange(FRAMES, dtype=jnp.int32)[:, None]
    seen_mask = jnp.logical_or(coin_flips < 3, frame_ids == anchor_frames[None, :]).astype(jnp.int32)
    return (seen_mask, anchor_frames)


def draw_visible(key, part):
    return track_layout(key)[0]


def draw_query_frame(key, part):
    return track_layout(key)[1]


def weight_pair(key, salt):
    first = jnp.clip(jax.random.normal(jax.random.fold_in(key, salt), (CHANNELS, CHANNELS), jnp.float32), -4.0, 4.0)
    second = jnp.clip(jax.random.normal(jax.random.fold_in(key, salt + 1), (CHANNELS, CHANNELS), jnp.float32), -4.0, 4.0)
    return (first, second)


def query_weight(key, salt):
    first, second = weight_pair(key, salt)
    return (2.0 * first / math.sqrt(CHANNELS)).astype(jnp.bfloat16)


def key_weight(key, salt):
    first, second = weight_pair(key, salt)
    mixed = second / math.sqrt(CHANNELS)
    return mixed.astype(jnp.bfloat16)


def draw_pixel_query(key, part):
    return query_weight(key, 601)


def draw_pixel_key(key, part):
    return key_weight(key, 601)


def draw_time_query(key, part):
    return query_weight(key, 611)


def draw_time_key(key, part):
    return key_weight(key, 611)


def block_levels(key, extent, shards, least, high):
    def one(dim, shards_of):
        steps = jax.random.uniform(jax.random.fold_in(jax.random.fold_in(key, 6), dim), (shards_of,), jnp.float32, least / len(shards), high / len(shards))
        return jnp.repeat(jnp.exp(steps), extent[dim] // shards_of).reshape((-1,) + (1,) * (len(extent) - dim - 1))

    loudness = one(*shards[0])
    for cut in shards[1:]:
        loudness = loudness * one(*cut)
    return loudness


def normal_values(rng, extent, spread, reach, held_as=jnp.bfloat16):
    values = jax.random.normal(rng, extent, jnp.float32) * spread
    return jnp.minimum(jnp.maximum(values, -reach), reach).astype(held_as)


def setup_inputs(seed: int = 0, part: int = 0) -> dict:
    seeds = jax.random.split(jax.random.key(seed), 16)
    own_keys = jax.random.split(jax.random.fold_in(seeds[15], part), 16)
    pixels = draw_pixels(jax.random.fold_in(jax.random.fold_in(seeds[15], part), 71), part)
    gru_state = jnp.clip(jax.random.uniform(own_keys[1], (FRAMES, ROWS, WIDTH, GRU_WIDTH), jnp.float32, -1.0, 1.0) * block_levels(own_keys[1], (FRAMES, ROWS, WIDTH, GRU_WIDTH), ((0, 8), (1, 2)), -0.4, 0.0), -1.0, 1.0).astype(jnp.bfloat16)
    tokens = draw_tokens(jax.random.fold_in(jax.random.fold_in(seeds[15], part), 71), part)
    visible = draw_visible(jax.random.fold_in(jax.random.fold_in(seeds[15], part), 71), part)
    query_frame = draw_query_frame(jax.random.fold_in(jax.random.fold_in(seeds[15], part), 71), part)
    pixel_query = draw_pixel_query(jax.random.fold_in(seeds[15], 71), part)
    pixel_key = draw_pixel_key(jax.random.fold_in(seeds[15], 71), part)
    pixel_value = normal_values(seeds[7], (CHANNELS, CHANNELS), CHANNELS ** -0.5, 0.375)
    pixel_out = normal_values(seeds[8], (CHANNELS, GRU_WIDTH), (CHANNELS // 16) ** -0.5, 1.5)
    time_query = draw_time_query(jax.random.fold_in(seeds[15], 71), part)
    time_key = draw_time_key(jax.random.fold_in(seeds[15], 71), part)
    time_value = normal_values(seeds[11], (CHANNELS, CHANNELS), CHANNELS ** -0.5, 0.375)
    time_out = normal_values(seeds[12], (CHANNELS, CHANNELS), (CHANNELS // 4) ** -0.5, 0.75)
    gru_gates = normal_values(seeds[13], (3, 3, 2 * GRU_WIDTH, 2 * GRU_WIDTH), (18 * GRU_WIDTH) ** -0.5, 0.125)
    gru_candidate = normal_values(seeds[14], (3, 3, 2 * GRU_WIDTH, GRU_WIDTH), (18 * GRU_WIDTH) ** -0.5, 0.125)
    return dict(pixels=pixels, gru_state=gru_state, tokens=tokens, visible=visible, query_frame=query_frame, pixel_query=pixel_query, pixel_key=pixel_key, pixel_value=pixel_value, pixel_out=pixel_out, time_query=time_query, time_key=time_key, time_value=time_value, time_out=time_out, gru_gates=gru_gates, gru_candidate=gru_candidate)


def attend_heads(queries, key_rows, value_rows, key_mask):
    score_scale = HEAD_DIM ** -0.5
    head_outputs = []
    for head_index in range(HEADS):
        offset = head_index * HEAD_DIM
        scores = jnp.dot(queries[:, offset:offset + HEAD_DIM], key_rows[:, offset:offset + HEAD_DIM].T, preferred_element_type=jnp.float32) * score_scale
        scores = jnp.where(key_mask[None, :], scores, -jnp.inf)
        weights = jax.nn.softmax(scores, axis=-1).astype(jnp.bfloat16)
        head_outputs.append(jnp.dot(weights, value_rows[:, offset:offset + HEAD_DIM], preferred_element_type=jnp.float32))
    return jnp.concatenate(head_outputs, axis=-1).astype(jnp.bfloat16)


def conv_rows(padded, weight, rows, columns):
    widened = jnp.pad(padded, ((0, 0), (1, 1), (0, 0)))
    summed = jnp.zeros((rows * columns, weight.shape[3]), jnp.float32)
    for row_shift in range(3):
        for col_shift in range(3):
            window = widened[row_shift:row_shift + rows, col_shift:col_shift + columns]
            summed = summed + jnp.dot(window.reshape(rows * columns, -1), weight[row_shift, col_shift], preferred_element_type=jnp.float32)
    return summed


def reference(pixels, gru_state, tokens, visible, query_frame, pixel_query, pixel_key, pixel_value, pixel_out, time_query, time_key, time_value, time_out, gru_gates, gru_candidate):
    def frame_context(inputs):
        frame_pixels, frame_tokens, frame_seen = inputs
        queries = jnp.dot(frame_pixels.reshape(ROWS * WIDTH, CHANNELS), pixel_query, preferred_element_type=jnp.float32).astype(jnp.bfloat16)
        key_rows = jnp.dot(frame_tokens, pixel_key, preferred_element_type=jnp.float32).astype(jnp.bfloat16)
        value_rows = jnp.dot(frame_tokens, pixel_value, preferred_element_type=jnp.float32).astype(jnp.bfloat16)
        attended = attend_heads(queries, key_rows, value_rows, frame_seen > 0)
        return jnp.dot(attended, pixel_out, preferred_element_type=jnp.float32).astype(jnp.bfloat16).reshape(ROWS, WIDTH, GRU_WIDTH)

    context = lax.map(frame_context, (pixels, tokens, visible))

    def frame_refine(inputs):
        state_now, context_now = inputs
        for iteration in range(ITERS):
            combined = jnp.concatenate([state_now, context_now], axis=-1)
            padded = jnp.pad(combined, ((1, 1), (0, 0), (0, 0)))
            gate_terms = conv_rows(padded, gru_gates, ROWS, WIDTH)
            update = jax.nn.sigmoid(gate_terms[:, :GRU_WIDTH])
            reset_gate = jax.nn.sigmoid(gate_terms[:, GRU_WIDTH:])
            state_flat = state_now.reshape(ROWS * WIDTH, GRU_WIDTH).astype(jnp.float32)
            reset_state = (reset_gate * state_flat).astype(jnp.bfloat16).reshape(ROWS, WIDTH, GRU_WIDTH)
            mixed_in = jnp.concatenate([reset_state, context_now], axis=-1)
            padded_mix = jnp.pad(mixed_in, ((1, 1), (0, 0), (0, 0)))
            candidate = jnp.tanh(conv_rows(padded_mix, gru_candidate, ROWS, WIDTH))
            state_now = ((1.0 - update) * state_flat + update * candidate).astype(jnp.bfloat16).reshape(ROWS, WIDTH, GRU_WIDTH)
        return state_now

    refined_state = lax.map(frame_refine, (gru_state, context))

    flat_tokens = tokens.reshape(FRAMES * TRACKS, CHANNELS)
    time_queries = jnp.dot(flat_tokens, time_query, preferred_element_type=jnp.float32).astype(jnp.bfloat16).reshape(FRAMES, TRACKS, CHANNELS)
    time_keys = jnp.dot(flat_tokens, time_key, preferred_element_type=jnp.float32).astype(jnp.bfloat16).reshape(FRAMES, TRACKS, CHANNELS)
    time_values = jnp.dot(flat_tokens, time_value, preferred_element_type=jnp.float32).astype(jnp.bfloat16).reshape(FRAMES, TRACKS, CHANNELS)
    anchor = time_queries[query_frame, jnp.arange(TRACKS)]
    joint_queries = (time_queries.astype(jnp.float32) + anchor.astype(jnp.float32)[None]).astype(jnp.bfloat16)
    shaped = (FRAMES, TRACKS, HEADS, HEAD_DIM)
    scores = jnp.einsum("fthd,gthd->thfg", joint_queries.astype(jnp.float32).reshape(shaped), time_keys.astype(jnp.float32).reshape(shaped)) * (HEAD_DIM ** -0.5)
    key_mask = jnp.transpose(visible) > 0
    scores = jnp.where(key_mask[:, None, None, :], scores, -jnp.inf)
    weights = jax.nn.softmax(scores, axis=-1).astype(jnp.bfloat16)
    attended = jnp.einsum("thfg,gthd->fthd", weights.astype(jnp.float32), time_values.astype(jnp.float32).reshape(shaped))
    time_attended = attended.astype(jnp.bfloat16).reshape(FRAMES * TRACKS, CHANNELS)
    projected = jnp.dot(time_attended, time_out, preferred_element_type=jnp.float32).reshape(FRAMES, TRACKS, CHANNELS)
    track_out = (tokens.astype(jnp.float32) + projected).astype(jnp.bfloat16)
    return refined_state, track_out
```

```python
import math

import jax
import jax.numpy as jnp
from jax import lax
from jax.experimental import pallas as pl
from jax.experimental.pallas import tpu as pltpu
from jax.sharding import PartitionSpec as P

HEADS = 8
HEAD_DIM = 32
GRU_WIDTH = 128
ITERS = 2
LOGIT_SCALE = HEAD_DIM ** (-0.5) * math.log2(math.e)
MASKED = -1e30
TILE = 8
LANES = 128
MESH = pl.DeviceIdType.MESH
F32 = jnp.float32
BF16 = jnp.bfloat16
N_IN = 15
UNROLL = 4
CHUNKS = 2


def dot(a, b):
    return jnp.dot(a, b, preferred_element_type=F32)


def dot_nt(a, b):
    return lax.dot_general(a, b, (((1,), (1,)), ((), ())), preferred_element_type=F32)


def iota(shape, dim):
    return lax.broadcasted_iota(jnp.int32, shape, dim)


def column_taps(x, columns):
    length = x.shape[0]
    col = lax.rem(iota(x.shape, 0), columns)
    left = jnp.where(col == 0, 0.0, pltpu.roll(x, 1, 0))
    right = jnp.where(col == columns - 1, 0.0, pltpu.roll(x, length - 1, 0))
    return jnp.concatenate([left.astype(BF16), x.astype(BF16), right.astype(BF16)], axis=1)


def interior_conv(x, w_ref, low, columns):
    width = x.shape[1]
    taps = column_taps(x, columns)
    zero = jnp.zeros((columns, taps.shape[1]), BF16)
    above = jnp.concatenate([zero, taps[:-columns]], axis=0)
    below = jnp.concatenate([taps[columns:], zero], axis=0)
    patches = jnp.concatenate([above, taps, below], axis=1)
    weight = w_ref[:, :, low : low + width, :]
    return dot(patches, weight.reshape(9 * width, weight.shape[3]))


def kernel(frames, bands, *refs):
    inputs, refs = refs[:N_IN], refs[N_IN:]
    (out_state, out_track), refs = refs[:2], refs[2:]
    (
        squares,
        pix,
        gst,
        tok,
        ints,
        wpo,
        wg,
        wc,
        partner_tok,
        partner_vis,
        tok_all,
        vis_all,
        queries,
        keys,
        values,
        att_out,
        returned,
        seen_bias,
        stages,
        halos,
        attended,
        tops,
        totals,
        acc_g,
        acc_c,
        ctx_g,
        ctx_c,
        state_new,
        track_new,
        load_sem,
        partner_send,
        partner_recv,
        tok_send,
        tok_recv,
        vis_send,
        vis_recv,
        back_send,
        back_recv,
        halo_send,
        halo_recv,
        out_sem,
    ) = refs
    (pix_h, gst_h, tok_h, vis_h, qfr_h) = inputs[:5]
    (wpq_h, wpk_h, wpv_h, wpo_h, wtq_h, wtk_h, wtv_h, wto_h, wg_h, wc_h) = inputs[5:]
    wpk, wpv, wpq, wtq, wtk, wtv, wto = [squares.at[i] for i in range(7)]
    vis, qfr = ints.at[0:1], ints.at[1:2]
    me = lax.axis_index("frame")
    band = lax.axis_index("band")
    other = lax.rem(band + 1, bands)
    tracks, channels = tok.shape[1], tok.shape[2]
    mine = tracks // frames
    chunks, part_rows = tok_all.shape[0], tok_all.shape[2]
    rows, columns = pix.shape[1], pix.shape[2]
    pixels = rows * columns

    barrier = pltpu.get_barrier_semaphore()
    for k in range(1, frames):
        pl.semaphore_signal(
            barrier, inc=1, device_id={"frame": lax.rem(me + k, frames)}, device_id_type=MESH
        )
    pl.semaphore_signal(barrier, inc=1, device_id={"band": other}, device_id_type=MESH)

    groups = (
        ((tok_h, tok), (wpk_h, wpk), (wpv_h, wpv)),
        ((pix_h, pix), (wpq_h, wpq)),
        ((vis_h, vis), (qfr_h, qfr)),
        ((wpo_h, wpo),),
        ((wtq_h, wtq), (wtk_h, wtk), (wtv_h, wtv), (wto_h, wto)),
        ((gst_h, gst),),
        ((wg_h, wg),),
        ((wc_h, wc),),
    )
    whole = (squares.at[0:4], squares.at[0:2], ints, wpo, squares.at[0:4], gst, wg, wc)
    for n, group in enumerate(groups):
        for src, dst in group:
            pltpu.make_async_copy(src, dst, load_sem.at[n]).start()

    def loaded(n):
        pltpu.make_async_copy(whole[n], whole[n], load_sem.at[n]).wait()

    def to_partner(src, dst, send, recv):
        return pltpu.make_async_remote_copy(
            src_ref=src,
            dst_ref=dst,
            send_sem=send,
            recv_sem=recv,
            device_id={"band": other},
            device_id_type=MESH,
        )

    def to_frame(target, src, dst, send, recv):
        return pltpu.make_async_remote_copy(
            src_ref=src,
            dst_ref=dst,
            send_sem=send,
            recv_sem=recv,
            device_id={"frame": target},
            device_id_type=MESH,
        )

    edge_row = (1 - band) * (rows - 1)
    edge = pl.multiple_of(edge_row * columns, columns)
    ring = sorted(range(1, frames), key=lambda k: -min(k, frames - k))

    def start_sends():
        with jax.named_scope("w_barrier"):
            pl.semaphore_wait(barrier, frames)
        to_partner(tok_h.at[0], partner_tok, partner_send, partner_recv.at[0]).start()
        to_partner(vis_h, partner_vis, vis_send, partner_recv.at[1]).start()
        for c in range(chunks):
            for k in ring:
                target = lax.rem(me + k, frames)
                start = pl.multiple_of(target * mine + c * part_rows, part_rows)
                rows_there = tok_h.at[0, pl.ds(start, part_rows)]
                to_frame(target, rows_there, tok_all.at[c, me], tok_send, tok_recv.at[c]).start()
            if c == 0:
                for k in ring:
                    target = lax.rem(me + k, frames)
                    to_frame(target, vis_h, vis_all.at[me], vis_send, vis_recv).start()
        for c in range(chunks):
            start = pl.multiple_of(me * mine + c * part_rows, part_rows)
            pltpu.make_async_copy(
                tok_h.at[0, pl.ds(start, part_rows)], tok_all.at[c, me], tok_recv.at[c]
            ).start()
        pltpu.make_async_copy(vis_h, vis_all.at[me], vis_recv).start()
        to_partner(gst_h.at[0, edge_row], halos.at[0], halo_send, halo_recv.at[0]).start()

    slot = jnp.where(me == 0, 2, jnp.where(me <= frames // 4, 1, 0))

    def at_slot(n):
        pl.when(slot == n)(start_sends)

    at_slot(0)
    with jax.named_scope("w_loads"):
        loaded(0)
    lane_head = lax.div(iota((1, channels), 1), HEAD_DIM)
    attended[...] = jnp.zeros_like(attended)
    tops[...] = jnp.zeros_like(tops)
    totals[...] = jnp.zeros_like(totals)

    def attend_half(half, track_rows, seen):
        keys[...] = dot(track_rows, wpk[...]).astype(BF16)
        values[...] = dot(track_rows, wpv[...]).astype(BF16)
        bias = jnp.where(seen > 0, 0.0, MASKED)

        def pixel_head(h, carry):
            chosen = jnp.where(lane_head == h, 1.0, 0.0)
            scores = dot_nt(queries[...] * chosen.astype(BF16), keys[...])
            scores = scores * LOGIT_SCALE + bias
            top = jnp.max(scores, axis=-1, keepdims=True)
            powers = jnp.exp2(scores - top)
            total = jnp.sum(powers, axis=-1, keepdims=True)
            tops[half] += top * chosen
            totals[half] += total * chosen
            attended[half] += dot(powers.astype(BF16), values[...]) * chosen
            return carry

        if half == 0:
            lax.fori_loop(0, HEADS // 2, pixel_head, 0, unroll=UNROLL)
            at_slot(1)
            lax.fori_loop(HEADS // 2, HEADS, pixel_head, 0, unroll=UNROLL)
            at_slot(2)
        else:
            lax.fori_loop(0, HEADS, pixel_head, 0, unroll=UNROLL)

    loaded(1)
    loaded(2)
    queries[...] = dot(pix[0].reshape(pixels, channels), wpq[...]).astype(BF16)

    with jax.named_scope("s_half0"):
        attend_half(0, tok[0], vis[...])
    with jax.named_scope("w_partner"):
        to_partner(tok_h.at[0], partner_tok, partner_send, partner_recv.at[0]).wait_recv()
        to_partner(vis_h, partner_vis, vis_send, partner_recv.at[1]).wait_recv()
    with jax.named_scope("s_half1"):
        attend_half(1, partner_tok[...], partner_vis[...])
    highest = jnp.maximum(tops[0], tops[1])
    share_0 = jnp.exp2(tops[0] - highest)
    share_1 = jnp.exp2(tops[1] - highest)
    merged = (attended[0] * share_0 + attended[1] * share_1) / (
        totals[0] * share_0 + totals[1] * share_1
    )
    loaded(3)
    context = dot(merged.astype(BF16), wpo[...]).astype(BF16)

    def share_edge(stage, value):
        stages[stage - 1, :, :] = value
        to_partner(
            stages.at[stage - 1, pl.ds(edge, columns)],
            halos.at[stage],
            halo_send,
            halo_recv.at[stage],
        ).start()

    def edge_here(stage):
        pltpu.make_async_copy(halos.at[stage], halos.at[stage], halo_recv.at[stage]).wait()

    share_edge(1, context)

    loaded(4)
    with jax.named_scope("w_vis"):
        pltpu.make_async_copy(vis_all, vis_all, vis_recv).wait()

    blocks = mine // TILE
    key_rows = HEADS * TILE
    pair = LANES // key_rows
    first_mine = me * mine
    picked = iota((tracks, mine), 0) == first_mine + iota((tracks, mine), 1)
    picked = jnp.where(picked, 1.0, 0.0).astype(BF16)
    seen_rows = vis_all[...].reshape(frames, tracks).astype(F32).astype(BF16)
    seen_mine = dot(seen_rows, picked).astype(BF16)
    spread_shape = (mine, blocks * LANES)
    slot = iota(spread_shape, 1)
    spread = iota(spread_shape, 0) == lax.div(slot, LANES) * TILE + lax.rem(slot, TILE)
    spread = jnp.where(spread, 1.0, 0.0).astype(BF16)
    hidden = (dot(seen_mine, spread) - 1.0) * -MASKED
    lane_slot = lax.div(iota((1, LANES), 1), key_rows)
    for g in range(0, frames, pair):
        row = hidden[g : g + 1]
        for k in range(1, pair):
            chosen = lax.rem(lax.div(iota(row.shape, 1), key_rows), pair) == k
            row = jnp.where(chosen, hidden[g + k : g + k + 1], row)
        seen_bias[g // pair : g // pair + 1, :] = row
    picked_rows = iota((mine, tracks), 1) == first_mine + iota((mine, tracks), 0)
    picked_rows = jnp.where(picked_rows, 1.0, 0.0).astype(BF16)
    query_rows = jnp.broadcast_to(qfr[...].astype(F32), (LANES, tracks)).astype(BF16)
    query_col = dot_nt(picked_rows, query_rows)
    same_track = iota((TILE, LANES), 0) == lax.rem(iota((TILE, LANES), 1), TILE)
    heads_half = LANES // HEAD_DIM
    head_masks = []
    for first in range(0, heads_half, 2):
        wanted = first + lax.div(iota((2 * TILE, LANES), 0), TILE)
        head_masks.append(
            jnp.where(lax.div(iota((2 * TILE, LANES), 1), HEAD_DIM) == wanted, 1.0, 0.0).astype(BF16)
        )
    empty = jnp.zeros((2 * TILE, LANES), BF16)
    halves = channels // LANES
    group = 2 * pair

    def by_head(values_32):
        doubled = jnp.concatenate([values_32, values_32], axis=0).astype(BF16)
        out = []
        for half in range(halves):
            part = doubled[:, half * LANES : (half + 1) * LANES]
            for mask in head_masks:
                pieces = [empty] * halves
                pieces[half] = part * mask
                out.append(jnp.concatenate(pieces, axis=1))
        return out

    def attend_time(c):
        with jax.named_scope("w_tok%d" % c):
            pltpu.make_async_copy(tok_all.at[c], tok_all.at[c], tok_recv.at[c]).wait()
        flat = tok_all[c].reshape(frames * part_rows, channels)
        t_q = dot(flat, wtq[...]).astype(BF16).astype(F32)
        t_k = dot(flat, wtk[...])
        t_v = dot(flat, wtv[...])
        results = []
        for tile in range(part_rows // TILE):
            block = c * (part_rows // TILE) + tile

            def frame_rows(x, f):
                return x[f * part_rows + tile * TILE : f * part_rows + (tile + 1) * TILE]

            asked = query_col[block * TILE : (block + 1) * TILE]
            asked = jnp.concatenate([asked] * halves, axis=1)
            q_frames = [frame_rows(t_q, f) for f in range(frames)]
            anchor = q_frames[0]
            for f in range(1, frames):
                anchor = jnp.where(asked == f, q_frames[f], anchor)
            joint = jnp.concatenate([q + anchor for q in q_frames], axis=0).astype(BF16)
            scores = []
            for g in range(0, frames, group):
                tile_keys = sum([by_head(frame_rows(t_k, g + k)) for k in range(group)], [])
                product = dot_nt(joint, jnp.concatenate(tile_keys, axis=0))
                for i in range(group // pair):
                    n = g // pair + i
                    bias = seen_bias[n : n + 1, block * LANES : (block + 1) * LANES]
                    scores.append(product[:, i * LANES : (i + 1) * LANES] * LOGIT_SCALE + bias)
            top = scores[0]
            for s in scores[1:]:
                top = jnp.maximum(top, s)
            for k in range(1, pair):
                top = jnp.maximum(top, pltpu.roll(top, k * key_rows, 1))
            powers = [jnp.exp2(s - top) for s in scores]
            total = powers[0]
            for p in powers[1:]:
                total = total + p
            turned = total
            for k in range(1, pair):
                total = total + pltpu.roll(turned, k * key_rows, 1)
            keep = jnp.concatenate([same_track] * frames, axis=0)
            inverse = jnp.where(keep, 1.0 / total, 0.0)
            weights = [(p * inverse).astype(BF16) for p in powers]
            result = None
            for g in range(0, frames, group):
                tile_values = sum([by_head(frame_rows(t_v, g + k)) for k in range(group)], [])
                first = g // pair
                part = dot(
                    jnp.concatenate(weights[first : first + group // pair], axis=1),
                    jnp.concatenate(tile_values, axis=0),
                )
                result = part if result is None else result + part
            results.append(result)
        for f in range(frames):
            att_out[c, f] = jnp.concatenate(
                [r[f * TILE : (f + 1) * TILE] for r in results], axis=0
            ).astype(BF16)
        for k in range(frames - 1):
            target = k + lax.div(k + frames - me, frames)
            to_frame(
                target, att_out.at[c, target], returned.at[c, me], back_send, back_recv.at[c]
            ).start()
        pltpu.make_async_copy(att_out.at[c, me], returned.at[c, me], back_recv.at[c]).start()

    for c in range(chunks):
        with jax.named_scope("s_time%d" % c):
            attend_time(c)

    def add_halo(acc, stage, w_ref, low):
        taps = column_taps(halos[stage].astype(F32), columns)
        weight = w_ref[pl.ds((1 - band) * 2, 1), :, low : low + GRU_WIDTH, :]
        weight = weight.reshape(3 * GRU_WIDTH, weight.shape[3])
        acc[pl.ds(edge, columns), :] += dot(taps, weight)

    for n in (5, 6, 7):
        loaded(n)
    context_f32 = context.astype(F32)
    with jax.named_scope("s_gctx"):
        ctx_g[...] = interior_conv(context_f32, wg, GRU_WIDTH, columns)
        ctx_c[...] = interior_conv(context_f32, wc, GRU_WIDTH, columns)
        edge_here(1)
        add_halo(ctx_g, 1, wg, GRU_WIDTH)
        add_halo(ctx_c, 1, wc, GRU_WIDTH)
    state = gst[0].reshape(pixels, GRU_WIDTH).astype(F32)
    state_stage = 0
    for iteration in range(ITERS):
        acc_g[...] = ctx_g[...] + interior_conv(state, wg, 0, columns)
        with jax.named_scope("w_hs%d" % iteration):
            edge_here(state_stage)
        add_halo(acc_g, state_stage, wg, 0)
        reset = jax.nn.sigmoid(acc_g[:, GRU_WIDTH:])
        reset_state = (reset * state).astype(BF16)
        share_edge(2 + 2 * iteration, reset_state)
        update = jax.nn.sigmoid(acc_g[:, :GRU_WIDTH])
        acc_c[...] = ctx_c[...] + interior_conv(reset_state.astype(F32), wc, 0, columns)
        with jax.named_scope("w_hr%d" % iteration):
            edge_here(2 + 2 * iteration)
        add_halo(acc_c, 2 + 2 * iteration, wc, 0)
        candidate = jnp.tanh(acc_c[...])
        new_state = ((1.0 - update) * state + update * candidate).astype(BF16)
        if iteration < ITERS - 1:
            state_stage = 3 + 2 * iteration
            share_edge(state_stage, new_state)
            state = new_state.astype(F32)
    state_new[...] = new_state.reshape(1, rows, columns, GRU_WIDTH)
    out_copies = [pltpu.make_async_copy(state_new, out_state, out_sem.at[0])]
    out_copies[0].start()

    for c in range(chunks):
        with jax.named_scope("w_back%d" % c):
            pltpu.make_async_copy(returned.at[c], returned.at[c], back_recv.at[c]).wait()
        with jax.named_scope("s_final%d" % c):
            update = dot(returned[c].reshape(frames * part_rows, channels), wto[...])
            for owner in range(frames):
                there = slice(owner * mine + c * part_rows, owner * mine + (c + 1) * part_rows)
                change = update[owner * part_rows : (owner + 1) * part_rows]
                track_new[0, there] = (tok[0, there].astype(F32) + change).astype(BF16)
    out_copies.append(pltpu.make_async_copy(track_new, out_track, out_sem.at[1]))
    out_copies[1].start()
    with jax.named_scope("w_out"):
        for copy in out_copies:
            copy.wait()
    with jax.named_scope("w_send"):
        sent = tok_all.at[:, 0 : frames - 1]
        to_partner(tok_h.at[0], partner_tok, partner_send, partner_recv.at[0]).wait_send()
        pltpu.make_async_copy(vis_all, vis_all, vis_send).wait()
        pltpu.make_async_copy(sent, sent, tok_send).wait()
        pltpu.make_async_copy(sent, sent, back_send).wait()
        pltpu.make_async_copy(halos, halos, halo_send).wait()


def deliver(state, track, out_state, out_track, sems):
    copies = [
        pltpu.make_async_copy(track, out_track, sems.at[0]),
        pltpu.make_async_copy(state, out_state, sems.at[1]),
    ]
    for copy in copies:
        copy.start()
    for copy in copies:
        copy.wait()


def on_device(frames, bands, *args):
    args = list(args)
    args[4] = args[4].reshape(1, -1)
    pixels, gru_state, tokens, visible = args[:4]
    tracks, channels = tokens.shape[1:]
    mine = tracks // frames
    chunks = CHUNKS if mine % (2 * CHUNKS * TILE) == 0 else 1
    part_rows = mine // chunks
    rows, columns = pixels.shape[1:3]
    count = rows * columns
    halo_stages = 1 + 2 * ITERS
    pair = LANES // (HEADS * TILE)
    dma = pltpu.SemaphoreType.DMA
    scratch = [
        pltpu.VMEM((7, channels, channels), BF16),
        pltpu.VMEM(pixels.shape, BF16),
        pltpu.VMEM(gru_state.shape, BF16),
        pltpu.VMEM(tokens.shape, BF16),
        pltpu.VMEM((2, tracks), jnp.int32),
        pltpu.VMEM(args[8].shape, BF16),
        pltpu.VMEM(args[13].shape, BF16),
        pltpu.VMEM(args[14].shape, BF16),
        pltpu.VMEM((tracks, channels), BF16),
        pltpu.VMEM((1, tracks), jnp.int32),
        pltpu.VMEM((chunks, frames, part_rows, channels), BF16),
        pltpu.VMEM((frames, 1, tracks), jnp.int32),
        pltpu.VMEM((count, channels), BF16),
        pltpu.VMEM((tracks, channels), BF16),
        pltpu.VMEM((tracks, channels), BF16),
        pltpu.VMEM((chunks, frames, part_rows, channels), BF16),
        pltpu.VMEM((chunks, frames, part_rows, channels), BF16),
        pltpu.VMEM((frames // pair, mine // TILE * LANES), F32),
        pltpu.VMEM((halo_stages - 1, count, GRU_WIDTH), BF16),
        pltpu.VMEM((halo_stages, columns, GRU_WIDTH), BF16),
        pltpu.VMEM((2, count, channels), F32),
        pltpu.VMEM((2, count, channels), F32),
        pltpu.VMEM((2, count, channels), F32),
        pltpu.VMEM((count, 2 * GRU_WIDTH), F32),
        pltpu.VMEM((count, GRU_WIDTH), F32),
        pltpu.VMEM((count, 2 * GRU_WIDTH), F32),
        pltpu.VMEM((count, GRU_WIDTH), F32),
        pltpu.VMEM(gru_state.shape, BF16),
        pltpu.VMEM(tokens.shape, BF16),
        dma((8,)),
        dma,
        dma((2,)),
        dma,
        dma((chunks,)),
        dma,
        dma,
        dma,
        dma((chunks,)),
        dma,
        dma((halo_stages,)),
        dma((2,)),
    ]

    def body(*refs):
        kernel(frames, bands, *refs)

    state, track = pl.pallas_call(
        body,
        out_shape=(
            pltpu.VMEM(gru_state.shape, BF16),
            pltpu.VMEM(tokens.shape, BF16),
        ),
        in_specs=[pl.BlockSpec(memory_space=pl.ANY)] * N_IN,
        out_specs=(pl.BlockSpec(memory_space=pl.ANY),) * 2,
        scratch_shapes=scratch,
        compiler_params=pltpu.CompilerParams(collective_id=0, has_side_effects=True),
        name="track_step",
    )(*args)
    return pl.pallas_call(
        deliver,
        out_shape=(
            jax.ShapeDtypeStruct(gru_state.shape, BF16),
            jax.ShapeDtypeStruct(tokens.shape, BF16),
        ),
        in_specs=[pl.BlockSpec(memory_space=pltpu.VMEM)] * 2,
        out_specs=(pl.BlockSpec(memory_space=pl.ANY),) * 2,
        scratch_shapes=[dma((2,))],
        name="track_deliver",
    )(pltpu.with_memory_space_constraint(state, pltpu.VMEM), pltpu.with_memory_space_constraint(track, pltpu.VMEM))


def solution(mesh):
    frames, bands = mesh.shape["frame"], mesh.shape["band"]
    placed = (
        P(("clip", "frame"), "band", None, None),
        P(("clip", "frame"), "band", None, None),
        P(("clip", "frame"), "band", None),
        P(("clip", "frame"), "band"),
        P(("clip", "band")),
    ) + (P(),) * 10
    return jax.shard_map(
        lambda *args: on_device(frames, bands, *args),
        mesh=mesh,
        in_specs=placed,
        out_specs=(P(("clip", "frame"), "band", None, None), P(("clip", "frame"), "band", None)),
        check_vma=False,
    )
```

```python
import math

import jax
import jax.numpy as jnp
from jax import lax
from jax.experimental import pallas as pl
from jax.experimental.pallas import tpu as pltpu
from jax.sharding import PartitionSpec as P

HEADS = 8
HEAD_DIM = 32
GRU_WIDTH = 128
ITERS = 2
LOGIT_SCALE = HEAD_DIM ** (-0.5) * math.log2(math.e)
MASKED = -1e30
TILE = 8
LANES = 128
MESH = pl.DeviceIdType.MESH
F32 = jnp.float32
BF16 = jnp.bfloat16
N_IN = 15
UNROLL = 4
CHUNKS = 2


def dot(a, b):
    return jnp.dot(a, b, preferred_element_type=F32)


def dot_nt(a, b):
    return lax.dot_general(a, b, (((1,), (1,)), ((), ())), preferred_element_type=F32)


def iota(shape, dim):
    return lax.broadcasted_iota(jnp.int32, shape, dim)


def column_taps(x, columns):
    length = x.shape[0]
    col = lax.rem(iota(x.shape, 0), columns)
    left = jnp.where(col == 0, 0.0, pltpu.roll(x, 1, 0))
    right = jnp.where(col == columns - 1, 0.0, pltpu.roll(x, length - 1, 0))
    return jnp.concatenate([left.astype(BF16), x.astype(BF16), right.astype(BF16)], axis=1)


def interior_conv(x, w_ref, low, columns):
    width = x.shape[1]
    taps = column_taps(x, columns)
    zero = jnp.zeros((columns, taps.shape[1]), BF16)
    above = jnp.concatenate([zero, taps[:-columns]], axis=0)
    below = jnp.concatenate([taps[columns:], zero], axis=0)
    patches = jnp.concatenate([above, taps, below], axis=1)
    weight = w_ref[:, :, low : low + width, :]
    return dot(patches, weight.reshape(9 * width, weight.shape[3]))


def kernel(frames, bands, *refs):
    inputs, refs = refs[:N_IN], refs[N_IN:]
    (out_state, out_track), refs = refs[:2], refs[2:]
    (
        squares,
        pix,
        gst,
        tok,
        ints,
        wpo,
        wg,
        wc,
        partner_tok,
        partner_vis,
        tok_all,
        vis_all,
        queries,
        keys,
        values,
        att_out,
        returned,
        seen_bias,
        stages,
        halos,
        attended,
        tops,
        totals,
        acc_g,
        acc_c,
        ctx_g,
        ctx_c,
        state_new,
        track_new,
        load_sem,
        partner_send,
        partner_recv,
        tok_send,
        tok_recv,
        vis_send,
        vis_recv,
        back_send,
        back_recv,
        halo_send,
        halo_recv,
        out_sem,
    ) = refs
    (pix_h, gst_h, tok_h, vis_h, qfr_h) = inputs[:5]
    (wpq_h, wpk_h, wpv_h, wpo_h, wtq_h, wtk_h, wtv_h, wto_h, wg_h, wc_h) = inputs[5:]
    wpk, wpv, wpq, wtq, wtk, wtv, wto = [squares.at[i] for i in range(7)]
    vis, qfr = ints.at[0:1], ints.at[1:2]
    me = lax.axis_index("frame")
    band = lax.axis_index("band")
    other = lax.rem(band + 1, bands)
    tracks, channels = tok.shape[1], tok.shape[2]
    mine = tracks // frames
    chunks, part_rows = tok_all.shape[0], tok_all.shape[2]
    rows, columns = pix.shape[1], pix.shape[2]
    pixels = rows * columns

    barrier = pltpu.get_barrier_semaphore()
    for k in range(1, frames):
        pl.semaphore_signal(
            barrier, inc=1, device_id={"frame": lax.rem(me + k, frames)}, device_id_type=MESH
        )
    pl.semaphore_signal(barrier, inc=1, device_id={"band": other}, device_id_type=MESH)

    groups = (
        ((tok_h, tok), (wpk_h, wpk), (wpv_h, wpv)),
        ((pix_h, pix), (wpq_h, wpq)),
        ((vis_h, vis), (qfr_h, qfr)),
        ((wpo_h, wpo),),
        ((wtq_h, wtq), (wtk_h, wtk), (wtv_h, wtv), (wto_h, wto)),
        ((gst_h, gst),),
        ((wg_h, wg),),
        ((wc_h, wc),),
    )
    whole = (squares.at[0:4], squares.at[0:2], ints, wpo, squares.at[0:4], gst, wg, wc)
    for n, group in enumerate(groups):
        for src, dst in group:
            pltpu.make_async_copy(src, dst, load_sem.at[n]).start()

    def loaded(n):
        pltpu.make_async_copy(whole[n], whole[n], load_sem.at[n]).wait()

    def to_partner(src, dst, send, recv):
        return pltpu.make_async_remote_copy(
            src_ref=src,
            dst_ref=dst,
            send_sem=send,
            recv_sem=recv,
            device_id={"band": other},
            device_id_type=MESH,
        )

    def to_frame(target, src, dst, send, recv):
        return pltpu.make_async_remote_copy(
            src_ref=src,
            dst_ref=dst,
            send_sem=send,
            recv_sem=recv,
            device_id={"frame": target},
            device_id_type=MESH,
        )

    edge_row = (1 - band) * (rows - 1)
    edge = pl.multiple_of(edge_row * columns, columns)
    ring = sorted(range(1, frames), key=lambda k: -min(k, frames - k))

    def start_sends():
        with jax.named_scope("w_barrier"):
            pl.semaphore_wait(barrier, frames)
        to_partner(tok_h.at[0], partner_tok, partner_send, partner_recv.at[0]).start()
        to_partner(vis_h, partner_vis, vis_send, partner_recv.at[1]).start()
        for k in ring:
            target = lax.rem(me + k, frames)
            to_frame(target, vis_h, vis_all.at[me], vis_send, vis_recv).start()
        for c in range(chunks):
            for k in ring:
                target = lax.rem(me + k, frames)
                start = pl.multiple_of(target * mine + c * part_rows, part_rows)
                rows_there = tok_h.at[0, pl.ds(start, part_rows)]
                to_frame(target, rows_there, tok_all.at[c, me], tok_send, tok_recv.at[c]).start()
        for c in range(chunks):
            start = pl.multiple_of(me * mine + c * part_rows, part_rows)
            pltpu.make_async_copy(
                tok_h.at[0, pl.ds(start, part_rows)], tok_all.at[c, me], tok_recv.at[c]
            ).start()
        pltpu.make_async_copy(vis_h, vis_all.at[me], vis_recv).start()
        to_partner(gst_h.at[0, edge_row], halos.at[0], halo_send, halo_recv.at[0]).start()

    slot = jnp.where(me == 0, 2, jnp.where(me <= frames // 4, 1, 0))

    def at_slot(n):
        pl.when(slot == n)(start_sends)

    at_slot(0)
    with jax.named_scope("w_loads"):
        loaded(0)
    def share_edge(stage, value):
        stages[stage - 1, :, :] = value
        to_partner(
            stages.at[stage - 1, pl.ds(edge, columns)],
            halos.at[stage],
            halo_send,
            halo_recv.at[stage],
        ).start()

    def edge_here(stage):
        pltpu.make_async_copy(halos.at[stage], halos.at[stage], halo_recv.at[stage]).wait()

    def add_halo(acc, stage, w_ref, low):
        taps = column_taps(halos[stage].astype(F32), columns)
        weight = w_ref[pl.ds((1 - band) * 2, 1), :, low : low + GRU_WIDTH, :]
        weight = weight.reshape(3 * GRU_WIDTH, weight.shape[3])
        acc[pl.ds(edge, columns), :] += dot(taps, weight)

    def gates_of_state(state, stage):
        acc_g[...] = interior_conv(state, wg, 0, columns)
        edge_here(stage)
        add_halo(acc_g, stage, wg, 0)

    def reset_of(state, stage):
        acc_g[...] += ctx_g[...]
        reset = jax.nn.sigmoid(acc_g[:, GRU_WIDTH:])
        reset_state = (reset * state).astype(BF16)
        share_edge(stage, reset_state)
        acc_c[...] = ctx_c[...] + interior_conv(reset_state.astype(F32), wc, 0, columns)

    def state_after(state, stage):
        update = jax.nn.sigmoid(acc_g[:, :GRU_WIDTH])
        with jax.named_scope("w_hr%d" % stage):
            edge_here(stage)
        add_halo(acc_c, stage, wc, 0)
        candidate = jnp.tanh(acc_c[...])
        return ((1.0 - update) * state + update * candidate).astype(BF16)

    lane_head = lax.div(iota((1, channels), 1), HEAD_DIM)
    attended[...] = jnp.zeros_like(attended)
    tops[...] = jnp.zeros_like(tops)
    totals[...] = jnp.zeros_like(totals)

    def attend_half(half, track_rows, seen):
        keys[...] = dot(track_rows, wpk[...]).astype(BF16)
        values[...] = dot(track_rows, wpv[...]).astype(BF16)
        bias = jnp.where(seen > 0, 0.0, MASKED)

        def pixel_head(h, carry):
            chosen = jnp.where(lane_head == h, 1.0, 0.0)
            scores = dot_nt(queries[...] * chosen.astype(BF16), keys[...])
            scores = scores * LOGIT_SCALE + bias
            top = jnp.max(scores, axis=-1, keepdims=True)
            powers = jnp.exp2(scores - top)
            total = jnp.sum(powers, axis=-1, keepdims=True)
            tops[half] += top * chosen
            totals[half] += total * chosen
            attended[half] += dot(powers.astype(BF16), values[...]) * chosen
            return carry

        if half == 0:
            lax.fori_loop(0, HEADS // 2, pixel_head, 0, unroll=UNROLL)
            at_slot(1)
            lax.fori_loop(HEADS // 2, HEADS, pixel_head, 0, unroll=UNROLL)
            at_slot(2)
        else:
            lax.fori_loop(0, HEADS, pixel_head, 0, unroll=UNROLL)

    loaded(1)
    loaded(2)
    queries[...] = dot(pix[0].reshape(pixels, channels), wpq[...]).astype(BF16)

    with jax.named_scope("s_half0"):
        attend_half(0, tok[0], vis[...])
    for n in (5, 6, 7):
        loaded(n)
    state = gst[0].reshape(pixels, GRU_WIDTH).astype(F32)
    with jax.named_scope("s_g0"):
        gates_of_state(state, 0)
    with jax.named_scope("w_partner"):
        to_partner(tok_h.at[0], partner_tok, partner_send, partner_recv.at[0]).wait_recv()
        to_partner(vis_h, partner_vis, vis_send, partner_recv.at[1]).wait_recv()
    with jax.named_scope("s_half1"):
        attend_half(1, partner_tok[...], partner_vis[...])
    highest = jnp.maximum(tops[0], tops[1])
    share_0 = jnp.exp2(tops[0] - highest)
    share_1 = jnp.exp2(tops[1] - highest)
    merged = (attended[0] * share_0 + attended[1] * share_1) / (
        totals[0] * share_0 + totals[1] * share_1
    )
    loaded(3)
    context = dot(merged.astype(BF16), wpo[...]).astype(BF16)

    share_edge(1, context)


    loaded(4)
    with jax.named_scope("w_vis"):
        pltpu.make_async_copy(vis_all, vis_all, vis_recv).wait()

    blocks = mine // TILE
    key_rows = HEADS * TILE
    pair = LANES // key_rows
    first_mine = me * mine
    picked = iota((tracks, mine), 0) == first_mine + iota((tracks, mine), 1)
    picked = jnp.where(picked, 1.0, 0.0).astype(BF16)
    seen_rows = vis_all[...].reshape(frames, tracks).astype(F32).astype(BF16)
    seen_mine = dot(seen_rows, picked).astype(BF16)
    spread_shape = (mine, blocks * LANES)
    slot = iota(spread_shape, 1)
    spread = iota(spread_shape, 0) == lax.div(slot, LANES) * TILE + lax.rem(slot, TILE)
    spread = jnp.where(spread, 1.0, 0.0).astype(BF16)
    hidden = (dot(seen_mine, spread) - 1.0) * -MASKED
    lane_slot = lax.div(iota((1, LANES), 1), key_rows)
    for g in range(0, frames, pair):
        row = hidden[g : g + 1]
        for k in range(1, pair):
            chosen = lax.rem(lax.div(iota(row.shape, 1), key_rows), pair) == k
            row = jnp.where(chosen, hidden[g + k : g + k + 1], row)
        seen_bias[g // pair : g // pair + 1, :] = row
    picked_rows = iota((mine, tracks), 1) == first_mine + iota((mine, tracks), 0)
    picked_rows = jnp.where(picked_rows, 1.0, 0.0).astype(BF16)
    query_rows = jnp.broadcast_to(qfr[...].astype(F32), (LANES, tracks)).astype(BF16)
    query_col = dot_nt(picked_rows, query_rows)
    same_track = iota((TILE, LANES), 0) == lax.rem(iota((TILE, LANES), 1), TILE)
    heads_half = LANES // HEAD_DIM
    head_masks = []
    for first in range(0, heads_half, 2):
        wanted = first + lax.div(iota((2 * TILE, LANES), 0), TILE)
        head_masks.append(
            jnp.where(lax.div(iota((2 * TILE, LANES), 1), HEAD_DIM) == wanted, 1.0, 0.0).astype(BF16)
        )
    empty = jnp.zeros((2 * TILE, LANES), BF16)
    halves = channels // LANES
    group = 2 * pair

    def by_head(values_32):
        doubled = jnp.concatenate([values_32, values_32], axis=0).astype(BF16)
        out = []
        for half in range(halves):
            part = doubled[:, half * LANES : (half + 1) * LANES]
            for mask in head_masks:
                pieces = [empty] * halves
                pieces[half] = part * mask
                out.append(jnp.concatenate(pieces, axis=1))
        return out

    def attend_time(c):
        with jax.named_scope("w_tok%d" % c):
            pltpu.make_async_copy(tok_all.at[c], tok_all.at[c], tok_recv.at[c]).wait()
        flat = tok_all[c].reshape(frames * part_rows, channels)
        t_q = dot(flat, wtq[...]).astype(BF16).astype(F32)
        t_k = dot(flat, wtk[...])
        t_v = dot(flat, wtv[...])
        tiles = range(part_rows // TILE)
        products = []
        for tile in tiles:

            def frame_rows(x, f):
                return x[f * part_rows + tile * TILE : f * part_rows + (tile + 1) * TILE]

            block = c * len(tiles) + tile
            asked = query_col[block * TILE : (block + 1) * TILE]
            asked = jnp.concatenate([asked] * halves, axis=1)
            q_frames = [frame_rows(t_q, f) for f in range(frames)]
            anchor = q_frames[0]
            for f in range(1, frames):
                anchor = jnp.where(asked == f, q_frames[f], anchor)
            joint = jnp.concatenate([q + anchor for q in q_frames], axis=0).astype(BF16)
            for g in range(0, frames, group):
                tile_keys = sum([by_head(frame_rows(t_k, g + k)) for k in range(group)], [])
                products.append(dot_nt(joint, jnp.concatenate(tile_keys, axis=0)))
        weights = []
        groups_of = frames // group
        for tile in tiles:
            block = c * len(tiles) + tile
            scores = []
            for n in range(frames // pair):
                product = products[tile * groups_of + n * pair // group]
                first = n * pair % group // pair * LANES
                bias = seen_bias[n : n + 1, block * LANES : (block + 1) * LANES]
                scores.append(product[:, first : first + LANES] * LOGIT_SCALE + bias)
            top = scores[0]
            for s in scores[1:]:
                top = jnp.maximum(top, s)
            turned = top
            for k in range(1, pair):
                top = jnp.maximum(top, pltpu.roll(turned, k * key_rows, 1))
            powers = [jnp.exp2(s - top) for s in scores]
            total = powers[0]
            for p in powers[1:]:
                total = total + p
            turned = total
            for k in range(1, pair):
                total = total + pltpu.roll(turned, k * key_rows, 1)
            keep = jnp.concatenate([same_track] * frames, axis=0)
            inverse = jnp.where(keep, 1.0 / total, 0.0)
            weights.append([(p * inverse).astype(BF16) for p in powers])
        results = []
        for tile in tiles:

            def frame_rows(x, f):
                return x[f * part_rows + tile * TILE : f * part_rows + (tile + 1) * TILE]

            tile_values = sum([by_head(frame_rows(t_v, f)) for f in range(frames)], [])
            results.append(
                dot(
                    jnp.concatenate(weights[tile], axis=1), jnp.concatenate(tile_values, axis=0)
                )
            )
        for f in range(frames):
            att_out[c, f] = jnp.concatenate(
                [r[f * TILE : (f + 1) * TILE] for r in results], axis=0
            ).astype(BF16)
        for k in range(frames - 1):
            target = k + lax.div(k + frames - me, frames)
            to_frame(
                target, att_out.at[c, target], returned.at[c, me], back_send, back_recv.at[c]
            ).start()
        pltpu.make_async_copy(att_out.at[c, me], returned.at[c, me], back_recv.at[c]).start()

    for c in range(chunks):
        with jax.named_scope("s_time%d" % c):
            attend_time(c)
    context_f32 = context.astype(F32)
    with jax.named_scope("s_gctx"):
        ctx_g[...] = interior_conv(context_f32, wg, GRU_WIDTH, columns)
        ctx_c[...] = interior_conv(context_f32, wc, GRU_WIDTH, columns)
    with jax.named_scope("w_hctx"):
        edge_here(1)
    add_halo(ctx_g, 1, wg, GRU_WIDTH)
    add_halo(ctx_c, 1, wc, GRU_WIDTH)
    with jax.named_scope("s_reset1"):
        reset_of(state, 2)
    with jax.named_scope("s_state1"):
        new_state = state_after(state, 2)
    share_edge(3, new_state)

    for iteration in range(1, ITERS):
        state = new_state.astype(F32)
        with jax.named_scope("s_g1"):
            gates_of_state(state, 1 + 2 * iteration)
            reset_of(state, 2 + 2 * iteration)
        with jax.named_scope("s_state2"):
            new_state = state_after(state, 2 + 2 * iteration)
        if iteration < ITERS - 1:
            share_edge(3 + 2 * iteration, new_state)
    state_new[...] = new_state.reshape(1, rows, columns, GRU_WIDTH)
    out_copies = [pltpu.make_async_copy(state_new, out_state, out_sem.at[0])]
    out_copies[0].start()

    for c in range(chunks):
        with jax.named_scope("w_back%d" % c):
            pltpu.make_async_copy(returned.at[c], returned.at[c], back_recv.at[c]).wait()
        with jax.named_scope("s_final%d" % c):
            update = dot(returned[c].reshape(frames * part_rows, channels), wto[...])
            for owner in range(frames):
                there = slice(owner * mine + c * part_rows, owner * mine + (c + 1) * part_rows)
                change = update[owner * part_rows : (owner + 1) * part_rows]
                track_new[0, there] = (tok[0, there].astype(F32) + change).astype(BF16)
    out_copies.append(pltpu.make_async_copy(track_new, out_track, out_sem.at[1]))
    out_copies[1].start()
    with jax.named_scope("w_out"):
        for copy in out_copies:
            copy.wait()
    with jax.named_scope("w_send"):
        sent = tok_all.at[:, 0 : frames - 1]
        to_partner(tok_h.at[0], partner_tok, partner_send, partner_recv.at[0]).wait_send()
        pltpu.make_async_copy(vis_all, vis_all, vis_send).wait()
        pltpu.make_async_copy(sent, sent, tok_send).wait()
        pltpu.make_async_copy(sent, sent, back_send).wait()
        pltpu.make_async_copy(halos, halos, halo_send).wait()


def deliver(state, track, out_state, out_track, sems):
    copies = [
        pltpu.make_async_copy(track, out_track, sems.at[0]),
        pltpu.make_async_copy(state, out_state, sems.at[1]),
    ]
    for copy in copies:
        copy.start()
    for copy in copies:
        copy.wait()


def on_device(frames, bands, *args):
    args = list(args)
    args[4] = args[4].reshape(1, -1)
    pixels, gru_state, tokens, visible = args[:4]
    tracks, channels = tokens.shape[1:]
    mine = tracks // frames
    chunks = CHUNKS if mine % (2 * CHUNKS * TILE) == 0 else 1
    part_rows = mine // chunks
    rows, columns = pixels.shape[1:3]
    count = rows * columns
    halo_stages = 1 + 2 * ITERS
    pair = LANES // (HEADS * TILE)
    dma = pltpu.SemaphoreType.DMA
    scratch = [
        pltpu.VMEM((7, channels, channels), BF16),
        pltpu.VMEM(pixels.shape, BF16),
        pltpu.VMEM(gru_state.shape, BF16),
        pltpu.VMEM(tokens.shape, BF16),
        pltpu.VMEM((2, tracks), jnp.int32),
        pltpu.VMEM(args[8].shape, BF16),
        pltpu.VMEM(args[13].shape, BF16),
        pltpu.VMEM(args[14].shape, BF16),
        pltpu.VMEM((tracks, channels), BF16),
        pltpu.VMEM((1, tracks), jnp.int32),
        pltpu.VMEM((chunks, frames, part_rows, channels), BF16),
        pltpu.VMEM((frames, 1, tracks), jnp.int32),
        pltpu.VMEM((count, channels), BF16),
        pltpu.VMEM((tracks, channels), BF16),
        pltpu.VMEM((tracks, channels), BF16),
        pltpu.VMEM((chunks, frames, part_rows, channels), BF16),
        pltpu.VMEM((chunks, frames, part_rows, channels), BF16),
        pltpu.VMEM((frames // pair, mine // TILE * LANES), F32),
        pltpu.VMEM((halo_stages - 1, count, GRU_WIDTH), BF16),
        pltpu.VMEM((halo_stages, columns, GRU_WIDTH), BF16),
        pltpu.VMEM((2, count, channels), F32),
        pltpu.VMEM((2, count, channels), F32),
        pltpu.VMEM((2, count, channels), F32),
        pltpu.VMEM((count, 2 * GRU_WIDTH), F32),
        pltpu.VMEM((count, GRU_WIDTH), F32),
        pltpu.VMEM((count, 2 * GRU_WIDTH), F32),
        pltpu.VMEM((count, GRU_WIDTH), F32),
        pltpu.VMEM(gru_state.shape, BF16),
        pltpu.VMEM(tokens.shape, BF16),
        dma((8,)),
        dma,
        dma((2,)),
        dma,
        dma((chunks,)),
        dma,
        dma,
        dma,
        dma((chunks,)),
        dma,
        dma((halo_stages,)),
        dma((2,)),
    ]

    def body(*refs):
        kernel(frames, bands, *refs)

    state, track = pl.pallas_call(
        body,
        out_shape=(
            pltpu.VMEM(gru_state.shape, BF16),
            pltpu.VMEM(tokens.shape, BF16),
        ),
        in_specs=[pl.BlockSpec(memory_space=pl.ANY)] * N_IN,
        out_specs=(pl.BlockSpec(memory_space=pl.ANY),) * 2,
        scratch_shapes=scratch,
        compiler_params=pltpu.CompilerParams(collective_id=0, has_side_effects=True),
        name="track_step",
    )(*args)
    return pl.pallas_call(
        deliver,
        out_shape=(
            jax.ShapeDtypeStruct(gru_state.shape, BF16),
            jax.ShapeDtypeStruct(tokens.shape, BF16),
        ),
        in_specs=[pl.BlockSpec(memory_space=pltpu.VMEM)] * 2,
        out_specs=(pl.BlockSpec(memory_space=pl.ANY),) * 2,
        scratch_shapes=[dma((2,))],
        name="track_deliver",
    )(pltpu.with_memory_space_constraint(state, pltpu.VMEM), pltpu.with_memory_space_constraint(track, pltpu.VMEM))


def solution(mesh):
    frames, bands = mesh.shape["frame"], mesh.shape["band"]
    placed = (
        P(("clip", "frame"), "band", None, None),
        P(("clip", "frame"), "band", None, None),
        P(("clip", "frame"), "band", None),
        P(("clip", "frame"), "band"),
        P(("clip", "band")),
    ) + (P(),) * 10
    return jax.shard_map(
        lambda *args: on_device(frames, bands, *args),
        mesh=mesh,
        in_specs=placed,
        out_specs=(P(("clip", "frame"), "band", None, None), P(("clip", "frame"), "band", None)),
        check_vma=False,
    )
```

```python
import math

import jax
import jax.numpy as jnp
from jax import lax
from jax.experimental import pallas as pl
from jax.experimental.pallas import tpu as pltpu
from jax.sharding import PartitionSpec as P

HEADS = 8
HEAD_DIM = 32
GRU_WIDTH = 128
ITERS = 2
LOGIT_SCALE = HEAD_DIM ** (-0.5) * math.log2(math.e)
MASKED = -1e30
TILE = 8
LANES = 128
MESH = pl.DeviceIdType.MESH
F32 = jnp.float32
BF16 = jnp.bfloat16
N_IN = 15
UNROLL = 4
CHUNKS = 2


def dot(a, b):
    return jnp.dot(a, b, preferred_element_type=F32)


def halves_dot(a, b):
    half = a.shape[0] // 2
    return jnp.concatenate([dot(a[:half], b), dot(a[half:], b)], axis=0)


def dot_nt(a, b):
    return lax.dot_general(a, b, (((1,), (1,)), ((), ())), preferred_element_type=F32)


def iota(shape, dim):
    return lax.broadcasted_iota(jnp.int32, shape, dim)


def column_taps(x, columns):
    length = x.shape[0]
    col = lax.rem(iota(x.shape, 0), columns)
    left = jnp.where(col == 0, 0.0, pltpu.roll(x, 1, 0))
    right = jnp.where(col == columns - 1, 0.0, pltpu.roll(x, length - 1, 0))
    return jnp.concatenate([left.astype(BF16), x.astype(BF16), right.astype(BF16)], axis=1)


def interior_conv(x, w_ref, low, columns):
    width = x.shape[1]
    taps = column_taps(x, columns)
    zero = jnp.zeros((columns, taps.shape[1]), BF16)
    above = jnp.concatenate([zero, taps[:-columns]], axis=0)
    below = jnp.concatenate([taps[columns:], zero], axis=0)
    patches = jnp.concatenate([above, taps, below], axis=1)
    weight = w_ref[:, :, low : low + width, :]
    return dot(patches, weight.reshape(9 * width, weight.shape[3]))


def kernel(frames, bands, *refs):
    inputs, refs = refs[:N_IN], refs[N_IN:]
    (out_state, out_track), refs = refs[:2], refs[2:]
    (
        squares,
        pix,
        gst,
        tok,
        ints,
        wpo,
        wg,
        wc,
        partner_tok,
        partner_vis,
        tok_all,
        vis_all,
        queries,
        keys,
        values,
        att_out,
        returned,
        seen_bias,
        stages,
        halos,
        attended,
        tops,
        totals,
        acc_g,
        acc_c,
        ctx_g,
        ctx_c,
        state_new,
        track_new,
        load_sem,
        partner_send,
        partner_recv,
        tok_send,
        tok_recv,
        vis_send,
        vis_recv,
        back_send,
        back_recv,
        halo_send,
        halo_recv,
        out_sem,
    ) = refs
    (pix_h, gst_h, tok_h, vis_h, qfr_h) = inputs[:5]
    (wpq_h, wpk_h, wpv_h, wpo_h, wtq_h, wtk_h, wtv_h, wto_h, wg_h, wc_h) = inputs[5:]
    wpk, wpv, wpq, wtq, wtk, wtv, wto = [squares.at[i] for i in range(7)]
    vis, qfr = ints.at[0:1], ints.at[1:2]
    me = lax.axis_index("frame")
    band = lax.axis_index("band")
    other = lax.rem(band + 1, bands)
    tracks, channels = tok.shape[1], tok.shape[2]
    mine = tracks // frames
    chunks, part_rows = tok_all.shape[0], tok_all.shape[2]
    rows, columns = pix.shape[1], pix.shape[2]
    pixels = rows * columns

    barrier = pltpu.get_barrier_semaphore()
    for k in range(1, frames):
        pl.semaphore_signal(
            barrier, inc=1, device_id={"frame": lax.rem(me + k, frames)}, device_id_type=MESH
        )
    pl.semaphore_signal(barrier, inc=1, device_id={"band": other}, device_id_type=MESH)

    groups = (
        ((tok_h, tok), (wpk_h, wpk), (wpv_h, wpv)),
        ((pix_h, pix), (wpq_h, wpq)),
        ((vis_h, vis), (qfr_h, qfr)),
        ((wpo_h, wpo),),
        ((wtq_h, wtq), (wtk_h, wtk), (wtv_h, wtv), (wto_h, wto)),
        ((gst_h, gst),),
        ((wg_h, wg),),
        ((wc_h, wc),),
    )
    whole = (squares.at[0:4], squares.at[0:2], ints, wpo, squares.at[0:4], gst, wg, wc)
    for n, group in enumerate(groups):
        for src, dst in group:
            pltpu.make_async_copy(src, dst, load_sem.at[n]).start()

    def loaded(n):
        pltpu.make_async_copy(whole[n], whole[n], load_sem.at[n]).wait()

    def to_partner(src, dst, send, recv):
        return pltpu.make_async_remote_copy(
            src_ref=src,
            dst_ref=dst,
            send_sem=send,
            recv_sem=recv,
            device_id={"band": other},
            device_id_type=MESH,
        )

    def to_frame(target, src, dst, send, recv):
        return pltpu.make_async_remote_copy(
            src_ref=src,
            dst_ref=dst,
            send_sem=send,
            recv_sem=recv,
            device_id={"frame": target},
            device_id_type=MESH,
        )

    edge_row = (1 - band) * (rows - 1)
    edge = pl.multiple_of(edge_row * columns, columns)
    ring = sorted(range(1, frames), key=lambda k: -min(k, frames - k))

    def send_tokens(parts):
        for c in parts:
            for k in ring:
                target = lax.rem(me + k, frames)
                start = pl.multiple_of(target * mine + c * part_rows, part_rows)
                rows_there = tok_h.at[0, pl.ds(start, part_rows)]
                to_frame(target, rows_there, tok_all.at[c, me], tok_send, tok_recv.at[c]).start()

    def send_rest():
        send_tokens(range(1, chunks))

    def start_sends():
        with jax.named_scope("w_barrier"):
            pl.semaphore_wait(barrier, frames)
        to_partner(tok_h.at[0], partner_tok, partner_send, partner_recv.at[0]).start()
        to_partner(vis_h, partner_vis, vis_send, partner_recv.at[1]).start()
        for k in ring:
            target = lax.rem(me + k, frames)
            to_frame(target, vis_h, vis_all.at[me], vis_send, vis_recv).start()
        send_tokens(range(1))
        pl.when(band == 0)(send_rest)
        for c in range(chunks):
            start = pl.multiple_of(me * mine + c * part_rows, part_rows)
            pltpu.make_async_copy(
                tok_h.at[0, pl.ds(start, part_rows)], tok_all.at[c, me], tok_recv.at[c]
            ).start()
        pltpu.make_async_copy(vis_h, vis_all.at[me], vis_recv).start()
        to_partner(gst_h.at[0, edge_row], halos.at[0], halo_send, halo_recv.at[0]).start()

    slot = jnp.where(me == 0, 2, jnp.where(me <= frames // 4, 1, 0))

    def at_slot(n):
        pl.when(slot == n)(start_sends)

    at_slot(0)
    with jax.named_scope("w_loads"):
        loaded(0)
    def share_edge(stage, value):
        stages[stage - 1, :, :] = value
        to_partner(
            stages.at[stage - 1, pl.ds(edge, columns)],
            halos.at[stage],
            halo_send,
            halo_recv.at[stage],
        ).start()

    def edge_here(stage):
        pltpu.make_async_copy(halos.at[stage], halos.at[stage], halo_recv.at[stage]).wait()

    def add_halo(acc, stage, w_ref, low):
        taps = column_taps(halos[stage].astype(F32), columns)
        weight = w_ref[pl.ds((1 - band) * 2, 1), :, low : low + GRU_WIDTH, :]
        weight = weight.reshape(3 * GRU_WIDTH, weight.shape[3])
        acc[pl.ds(edge, columns), :] += dot(taps, weight)

    def gates_of_state(state, stage):
        acc_g[...] = interior_conv(state, wg, 0, columns)
        edge_here(stage)
        add_halo(acc_g, stage, wg, 0)

    def reset_of(state, stage):
        acc_g[...] += ctx_g[...]
        reset = jax.nn.sigmoid(acc_g[:, GRU_WIDTH:])
        reset_state = (reset * state).astype(BF16)
        share_edge(stage, reset_state)
        acc_c[...] = ctx_c[...] + interior_conv(reset_state.astype(F32), wc, 0, columns)

    def state_after(state, stage):
        update = jax.nn.sigmoid(acc_g[:, :GRU_WIDTH])
        with jax.named_scope("w_hr%d" % stage):
            edge_here(stage)
        add_halo(acc_c, stage, wc, 0)
        candidate = jnp.tanh(acc_c[...])
        return ((1.0 - update) * state + update * candidate).astype(BF16)

    lane_head = lax.div(iota((1, channels), 1), HEAD_DIM)
    attended[...] = jnp.zeros_like(attended)
    tops[...] = jnp.zeros_like(tops)
    totals[...] = jnp.zeros_like(totals)

    def attend_half(half, track_rows, seen):
        keys[...] = dot(track_rows, wpk[...]).astype(BF16)
        values[...] = dot(track_rows, wpv[...]).astype(BF16)
        bias = jnp.where(seen > 0, 0.0, MASKED)

        def pixel_head(h, carry):
            chosen = jnp.where(lane_head == h, 1.0, 0.0)
            scores = dot_nt(queries[...] * chosen.astype(BF16), keys[...])
            scores = scores * LOGIT_SCALE + bias
            top = jnp.max(scores, axis=-1, keepdims=True)
            powers = jnp.exp2(scores - top)
            total = jnp.sum(powers, axis=-1, keepdims=True)
            tops[half] += top * chosen
            totals[half] += total * chosen
            attended[half] += dot(powers.astype(BF16), values[...]) * chosen
            return carry

        if half == 0:
            lax.fori_loop(0, HEADS // 2, pixel_head, 0, unroll=UNROLL)
            at_slot(1)
            lax.fori_loop(HEADS // 2, HEADS, pixel_head, 0, unroll=UNROLL)
            at_slot(2)
        else:
            lax.fori_loop(0, HEADS // 2, pixel_head, 0, unroll=UNROLL)
            pl.when(band > 0)(send_rest)
            lax.fori_loop(HEADS // 2, HEADS, pixel_head, 0, unroll=UNROLL)

    loaded(1)
    loaded(2)
    queries[...] = dot(pix[0].reshape(pixels, channels), wpq[...]).astype(BF16)

    with jax.named_scope("s_half0"):
        attend_half(0, tok[0], vis[...])
    for n in (5, 6, 7):
        loaded(n)
    state = gst[0].reshape(pixels, GRU_WIDTH).astype(F32)
    with jax.named_scope("s_g0"):
        gates_of_state(state, 0)
    with jax.named_scope("w_partner"):
        to_partner(tok_h.at[0], partner_tok, partner_send, partner_recv.at[0]).wait_recv()
        to_partner(vis_h, partner_vis, vis_send, partner_recv.at[1]).wait_recv()
    with jax.named_scope("s_half1"):
        attend_half(1, partner_tok[...], partner_vis[...])
    highest = jnp.maximum(tops[0], tops[1])
    share_0 = jnp.exp2(tops[0] - highest)
    share_1 = jnp.exp2(tops[1] - highest)
    merged = (attended[0] * share_0 + attended[1] * share_1) / (
        totals[0] * share_0 + totals[1] * share_1
    )
    loaded(3)
    context = dot(merged.astype(BF16), wpo[...]).astype(BF16)

    share_edge(1, context)


    loaded(4)
    with jax.named_scope("w_vis"):
        pltpu.make_async_copy(vis_all, vis_all, vis_recv).wait()

    blocks = mine // TILE
    key_rows = HEADS * TILE
    pair = LANES // key_rows
    first_mine = me * mine
    picked = iota((tracks, mine), 0) == first_mine + iota((tracks, mine), 1)
    picked = jnp.where(picked, 1.0, 0.0).astype(BF16)
    seen_rows = vis_all[...].reshape(frames, tracks).astype(F32).astype(BF16)
    seen_mine = dot(seen_rows, picked).astype(BF16)
    spread_shape = (mine, blocks * LANES)
    slot = iota(spread_shape, 1)
    spread = iota(spread_shape, 0) == lax.div(slot, LANES) * TILE + lax.rem(slot, TILE)
    spread = jnp.where(spread, 1.0, 0.0).astype(BF16)
    hidden = (dot(seen_mine, spread) - 1.0) * -MASKED
    lane_slot = lax.div(iota((1, LANES), 1), key_rows)
    for g in range(0, frames, pair):
        row = hidden[g : g + 1]
        for k in range(1, pair):
            chosen = lax.rem(lax.div(iota(row.shape, 1), key_rows), pair) == k
            row = jnp.where(chosen, hidden[g + k : g + k + 1], row)
        seen_bias[g // pair : g // pair + 1, :] = row
    picked_rows = iota((mine, tracks), 1) == first_mine + iota((mine, tracks), 0)
    picked_rows = jnp.where(picked_rows, 1.0, 0.0).astype(BF16)
    query_rows = jnp.broadcast_to(qfr[...].astype(F32), (LANES, tracks)).astype(BF16)
    query_col = dot_nt(picked_rows, query_rows)
    same_track = iota((TILE, LANES), 0) == lax.rem(iota((TILE, LANES), 1), TILE)
    heads_half = LANES // HEAD_DIM
    head_masks = []
    for first in range(0, heads_half, 2):
        wanted = first + lax.div(iota((2 * TILE, LANES), 0), TILE)
        head_masks.append(
            jnp.where(lax.div(iota((2 * TILE, LANES), 1), HEAD_DIM) == wanted, 1.0, 0.0).astype(BF16)
        )
    empty = jnp.zeros((2 * TILE, LANES), BF16)
    halves = channels // LANES
    group = 2 * pair

    def by_head(values_32):
        doubled = jnp.concatenate([values_32, values_32], axis=0).astype(BF16)
        out = []
        for half in range(halves):
            part = doubled[:, half * LANES : (half + 1) * LANES]
            for mask in head_masks:
                pieces = [empty] * halves
                pieces[half] = part * mask
                out.append(jnp.concatenate(pieces, axis=1))
        return out

    late = range(frames // 4, frames // 2)
    back_order = [[] for _ in range(chunks)]
    for c in range(chunks - 1):
        back_order[c] = [(c, n) for n in range(frames - 1) if n not in late]
    back_order[-1] = [(chunks - 1, n) for n in range(frames // 4)]
    back_order[-1] += [(c, n) for c in range(chunks - 1) for n in range(frames - 1) if n in late]
    back_order[-1] += [(chunks - 1, n) for n in range(frames // 4, frames - 1)]

    def attend_time(c):
        with jax.named_scope("w_tok%d" % c):
            pltpu.make_async_copy(tok_all.at[c], tok_all.at[c], tok_recv.at[c]).wait()
        flat = tok_all[c].reshape(frames * part_rows, channels)
        t_q = dot(flat, wtq[...]).astype(BF16).astype(F32)
        t_k = dot(flat, wtk[...])
        t_v = halves_dot(flat, wtv[...])
        tiles = range(part_rows // TILE)
        products = []
        for tile in tiles:

            def frame_rows(x, f):
                return x[f * part_rows + tile * TILE : f * part_rows + (tile + 1) * TILE]

            block = c * len(tiles) + tile
            asked = query_col[block * TILE : (block + 1) * TILE]
            asked = jnp.concatenate([asked] * halves, axis=1)
            q_frames = [frame_rows(t_q, f) for f in range(frames)]
            anchor = q_frames[0]
            for f in range(1, frames):
                anchor = jnp.where(asked == f, q_frames[f], anchor)
            joint = jnp.concatenate([q + anchor for q in q_frames], axis=0).astype(BF16)
            for g in range(0, frames, group):
                tile_keys = sum([by_head(frame_rows(t_k, g + k)) for k in range(group)], [])
                products.append(dot_nt(joint, jnp.concatenate(tile_keys, axis=0)))
        weights = []
        groups_of = frames // group
        for tile in tiles:
            block = c * len(tiles) + tile
            scores = []
            for n in range(frames // pair):
                product = products[tile * groups_of + n * pair // group]
                first = n * pair % group // pair * LANES
                bias = seen_bias[n : n + 1, block * LANES : (block + 1) * LANES]
                scores.append(product[:, first : first + LANES] * LOGIT_SCALE + bias)
            top = scores[0]
            for s in scores[1:]:
                top = jnp.maximum(top, s)
            turned = top
            for k in range(1, pair):
                top = jnp.maximum(top, pltpu.roll(turned, k * key_rows, 1))
            powers = [jnp.exp2(s - top) for s in scores]
            total = powers[0]
            for p in powers[1:]:
                total = total + p
            turned = total
            for k in range(1, pair):
                total = total + pltpu.roll(turned, k * key_rows, 1)
            keep = jnp.concatenate([same_track] * frames, axis=0)
            inverse = jnp.where(keep, 1.0 / total, 0.0)
            weights.append([(p * inverse).astype(BF16) for p in powers])
        results = []
        for tile in tiles:

            def frame_rows(x, f):
                return x[f * part_rows + tile * TILE : f * part_rows + (tile + 1) * TILE]

            tile_values = sum([by_head(frame_rows(t_v, f)) for f in range(frames)], [])
            results.append(
                dot(
                    jnp.concatenate(weights[tile], axis=1), jnp.concatenate(tile_values, axis=0)
                )
            )
        for f in range(frames):
            att_out[c, f] = jnp.concatenate(
                [r[f * TILE : (f + 1) * TILE] for r in results], axis=0
            ).astype(BF16)
        pltpu.make_async_copy(att_out.at[c, me], returned.at[c, me], back_recv.at[c]).start()
        for part, n in back_order[c]:
            target = n + lax.div(n + frames - me, frames)
            to_frame(
                target,
                att_out.at[part, target],
                returned.at[part, me],
                back_send,
                back_recv.at[part],
            ).start()

    for c in range(chunks):
        with jax.named_scope("s_time%d" % c):
            attend_time(c)
    context_f32 = context.astype(F32)
    with jax.named_scope("s_gctx"):
        ctx_g[...] = interior_conv(context_f32, wg, GRU_WIDTH, columns)
        ctx_c[...] = interior_conv(context_f32, wc, GRU_WIDTH, columns)
    with jax.named_scope("w_hctx"):
        edge_here(1)
    add_halo(ctx_g, 1, wg, GRU_WIDTH)
    add_halo(ctx_c, 1, wc, GRU_WIDTH)
    with jax.named_scope("s_reset1"):
        reset_of(state, 2)
    with jax.named_scope("s_state1"):
        new_state = state_after(state, 2)
    share_edge(3, new_state)

    for iteration in range(1, ITERS):
        state = new_state.astype(F32)
        with jax.named_scope("s_g1"):
            gates_of_state(state, 1 + 2 * iteration)
            reset_of(state, 2 + 2 * iteration)
        with jax.named_scope("s_state2"):
            new_state = state_after(state, 2 + 2 * iteration)
        if iteration < ITERS - 1:
            share_edge(3 + 2 * iteration, new_state)
    state_new[...] = new_state.reshape(1, rows, columns, GRU_WIDTH)
    out_copies = [pltpu.make_async_copy(state_new, out_state, out_sem.at[0])]
    out_copies[0].start()

    for c in range(chunks):
        with jax.named_scope("w_back%d" % c):
            pltpu.make_async_copy(returned.at[c], returned.at[c], back_recv.at[c]).wait()
        with jax.named_scope("s_final%d" % c):
            update = halves_dot(returned[c].reshape(frames * part_rows, channels), wto[...])
            for owner in range(frames):
                there = slice(owner * mine + c * part_rows, owner * mine + (c + 1) * part_rows)
                change = update[owner * part_rows : (owner + 1) * part_rows]
                track_new[0, there] = (tok[0, there].astype(F32) + change).astype(BF16)
    out_copies.append(pltpu.make_async_copy(track_new, out_track, out_sem.at[1]))
    out_copies[1].start()
    with jax.named_scope("w_out"):
        for copy in out_copies:
            copy.wait()
    with jax.named_scope("w_send"):
        sent = tok_all.at[:, 0 : frames - 1]
        to_partner(tok_h.at[0], partner_tok, partner_send, partner_recv.at[0]).wait_send()
        pltpu.make_async_copy(vis_all, vis_all, vis_send).wait()
        pltpu.make_async_copy(sent, sent, tok_send).wait()
        pltpu.make_async_copy(sent, sent, back_send).wait()
        pltpu.make_async_copy(halos, halos, halo_send).wait()


def deliver(state, track, out_state, out_track, sems):
    copies = [
        pltpu.make_async_copy(track, out_track, sems.at[0]),
        pltpu.make_async_copy(state, out_state, sems.at[1]),
    ]
    for copy in copies:
        copy.start()
    for copy in copies:
        copy.wait()


def on_device(frames, bands, *args):
    args = list(args)
    args[4] = args[4].reshape(1, -1)
    pixels, gru_state, tokens, visible = args[:4]
    tracks, channels = tokens.shape[1:]
    mine = tracks // frames
    chunks = CHUNKS if mine % (2 * CHUNKS * TILE) == 0 else 1
    part_rows = mine // chunks
    rows, columns = pixels.shape[1:3]
    count = rows * columns
    halo_stages = 1 + 2 * ITERS
    pair = LANES // (HEADS * TILE)
    dma = pltpu.SemaphoreType.DMA
    scratch = [
        pltpu.VMEM((7, channels, channels), BF16),
        pltpu.VMEM(pixels.shape, BF16),
        pltpu.VMEM(gru_state.shape, BF16),
        pltpu.VMEM(tokens.shape, BF16),
        pltpu.VMEM((2, tracks), jnp.int32),
        pltpu.VMEM(args[8].shape, BF16),
        pltpu.VMEM(args[13].shape, BF16),
        pltpu.VMEM(args[14].shape, BF16),
        pltpu.VMEM((tracks, channels), BF16),
        pltpu.VMEM((1, tracks), jnp.int32),
        pltpu.VMEM((chunks, frames, part_rows, channels), BF16),
        pltpu.VMEM((frames, 1, tracks), jnp.int32),
        pltpu.VMEM((count, channels), BF16),
        pltpu.VMEM((tracks, channels), BF16),
        pltpu.VMEM((tracks, channels), BF16),
        pltpu.VMEM((chunks, frames, part_rows, channels), BF16),
        pltpu.VMEM((chunks, frames, part_rows, channels), BF16),
        pltpu.VMEM((frames // pair, mine // TILE * LANES), F32),
        pltpu.VMEM((halo_stages - 1, count, GRU_WIDTH), BF16),
        pltpu.VMEM((halo_stages, columns, GRU_WIDTH), BF16),
        pltpu.VMEM((2, count, channels), F32),
        pltpu.VMEM((2, count, channels), F32),
        pltpu.VMEM((2, count, channels), F32),
        pltpu.VMEM((count, 2 * GRU_WIDTH), F32),
        pltpu.VMEM((count, GRU_WIDTH), F32),
        pltpu.VMEM((count, 2 * GRU_WIDTH), F32),
        pltpu.VMEM((count, GRU_WIDTH), F32),
        pltpu.VMEM(gru_state.shape, BF16),
        pltpu.VMEM(tokens.shape, BF16),
        dma((8,)),
        dma,
        dma((2,)),
        dma,
        dma((chunks,)),
        dma,
        dma,
        dma,
        dma((chunks,)),
        dma,
        dma((halo_stages,)),
        dma((2,)),
    ]

    def body(*refs):
        kernel(frames, bands, *refs)

    state, track = pl.pallas_call(
        body,
        out_shape=(
            pltpu.VMEM(gru_state.shape, BF16),
            pltpu.VMEM(tokens.shape, BF16),
        ),
        in_specs=[pl.BlockSpec(memory_space=pl.ANY)] * N_IN,
        out_specs=(pl.BlockSpec(memory_space=pl.ANY),) * 2,
        scratch_shapes=scratch,
        compiler_params=pltpu.CompilerParams(collective_id=0, has_side_effects=True),
        name="track_step",
    )(*args)
    return pl.pallas_call(
        deliver,
        out_shape=(
            jax.ShapeDtypeStruct(gru_state.shape, BF16),
            jax.ShapeDtypeStruct(tokens.shape, BF16),
        ),
        in_specs=[pl.BlockSpec(memory_space=pltpu.VMEM)] * 2,
        out_specs=(pl.BlockSpec(memory_space=pl.ANY),) * 2,
        scratch_shapes=[dma((2,))],
        name="track_deliver",
    )(pltpu.with_memory_space_constraint(state, pltpu.VMEM), pltpu.with_memory_space_constraint(track, pltpu.VMEM))


def solution(mesh):
    frames, bands = mesh.shape["frame"], mesh.shape["band"]
    placed = (
        P(("clip", "frame"), "band", None, None),
        P(("clip", "frame"), "band", None, None),
        P(("clip", "frame"), "band", None),
        P(("clip", "frame"), "band"),
        P(("clip", "band")),
    ) + (P(),) * 10
    return jax.shard_map(
        lambda *args: on_device(frames, bands, *args),
        mesh=mesh,
        in_specs=placed,
        out_specs=(P(("clip", "frame"), "band", None, None), P(("clip", "frame"), "band", None)),
        check_vma=False,
    )
```

```python
import math

import jax
import jax.numpy as jnp
from jax import lax
from jax.experimental import pallas as pl
from jax.experimental.pallas import tpu as pltpu
from jax.sharding import PartitionSpec as P

HEADS = 8
HEAD_DIM = 32
GRU_WIDTH = 128
ITERS = 2
LOGIT_SCALE = HEAD_DIM ** (-0.5) * math.log2(math.e)
MASKED = -1e30
TILE = 8
LANES = 128
MESH = pl.DeviceIdType.MESH
F32 = jnp.float32
BF16 = jnp.bfloat16
N_IN = 15
UNROLL = 4
CHUNKS = 2


def dot(a, b):
    return jnp.dot(a, b, preferred_element_type=F32)


def halves_dot(a, b):
    half = a.shape[0] // 2
    return jnp.concatenate([dot(a[:half], b), dot(a[half:], b)], axis=0)


def dot_nt(a, b):
    return lax.dot_general(a, b, (((1,), (1,)), ((), ())), preferred_element_type=F32)


def iota(shape, dim):
    return lax.broadcasted_iota(jnp.int32, shape, dim)


def column_taps(x, columns):
    length = x.shape[0]
    col = lax.rem(iota(x.shape, 0), columns)
    left = jnp.where(col == 0, 0.0, pltpu.roll(x, 1, 0))
    right = jnp.where(col == columns - 1, 0.0, pltpu.roll(x, length - 1, 0))
    return jnp.concatenate([left.astype(BF16), x.astype(BF16), right.astype(BF16)], axis=1)


def interior_conv(x, w_ref, low, columns):
    width = x.shape[1]
    taps = column_taps(x, columns)
    zero = jnp.zeros((columns, taps.shape[1]), BF16)
    above = jnp.concatenate([zero, taps[:-columns]], axis=0)
    below = jnp.concatenate([taps[columns:], zero], axis=0)
    patches = jnp.concatenate([above, taps, below], axis=1)
    weight = w_ref[:, :, low : low + width, :]
    return dot(patches, weight.reshape(9 * width, weight.shape[3]))


def kernel(frames, bands, *refs):
    inputs, refs = refs[:N_IN], refs[N_IN:]
    (out_state, out_track), refs = refs[:2], refs[2:]
    (
        squares,
        pix,
        gst,
        tok,
        ints,
        wpo,
        wg,
        wc,
        partner_tok,
        partner_vis,
        tok_all,
        vis_all,
        queries,
        keys,
        values,
        att_out,
        returned,
        seen_bias,
        stages,
        halos,
        attended,
        tops,
        totals,
        acc_g,
        acc_c,
        ctx_g,
        ctx_c,
        state_new,
        track_new,
        load_sem,
        partner_send,
        partner_recv,
        tok_send,
        tok_recv,
        vis_send,
        vis_recv,
        back_send,
        back_recv,
        halo_send,
        halo_recv,
        out_sem,
    ) = refs
    (pix_h, gst_h, tok_h, vis_h, qfr_h) = inputs[:5]
    (wpq_h, wpk_h, wpv_h, wpo_h, wtq_h, wtk_h, wtv_h, wto_h, wg_h, wc_h) = inputs[5:]
    wpk, wpv, wpq, wtq, wtk, wtv, wto = [squares.at[i] for i in range(7)]
    vis, qfr = ints.at[0:1], ints.at[1:2]
    me = lax.axis_index("frame")
    band = lax.axis_index("band")
    other = lax.rem(band + 1, bands)
    tracks, channels = tok.shape[1], tok.shape[2]
    mine = tracks // frames
    chunks, part_rows = tok_all.shape[0], tok_all.shape[2]
    rows, columns = pix.shape[1], pix.shape[2]
    pixels = rows * columns

    barrier = pltpu.get_barrier_semaphore()
    for k in range(1, frames):
        pl.semaphore_signal(
            barrier, inc=1, device_id={"frame": lax.rem(me + k, frames)}, device_id_type=MESH
        )
    pl.semaphore_signal(barrier, inc=1, device_id={"band": other}, device_id_type=MESH)

    groups = (
        ((tok_h, tok), (wpk_h, wpk), (wpv_h, wpv)),
        ((pix_h, pix), (wpq_h, wpq)),
        ((vis_h, vis), (qfr_h, qfr)),
        ((wpo_h, wpo),),
        ((wtq_h, wtq), (wtk_h, wtk), (wtv_h, wtv), (wto_h, wto)),
        ((gst_h, gst),),
        ((wg_h, wg),),
        ((wc_h, wc),),
    )
    whole = (squares.at[0:4], squares.at[0:2], ints, wpo, squares.at[0:4], gst, wg, wc)
    for n, group in enumerate(groups):
        for src, dst in group:
            pltpu.make_async_copy(src, dst, load_sem.at[n]).start()

    def loaded(n):
        pltpu.make_async_copy(whole[n], whole[n], load_sem.at[n]).wait()

    def to_partner(src, dst, send, recv):
        return pltpu.make_async_remote_copy(
            src_ref=src,
            dst_ref=dst,
            send_sem=send,
            recv_sem=recv,
            device_id={"band": other},
            device_id_type=MESH,
        )

    def to_frame(target, src, dst, send, recv):
        return pltpu.make_async_remote_copy(
            src_ref=src,
            dst_ref=dst,
            send_sem=send,
            recv_sem=recv,
            device_id={"frame": target},
            device_id_type=MESH,
        )

    edge_row = (1 - band) * (rows - 1)
    edge = pl.multiple_of(edge_row * columns, columns)
    ring = sorted(range(1, frames), key=lambda k: -min(k, frames - k))

    def send_tokens(parts):
        for c in parts:
            for k in ring:
                target = lax.rem(me + k, frames)
                start = pl.multiple_of(target * mine + c * part_rows, part_rows)
                rows_there = tok_h.at[0, pl.ds(start, part_rows)]
                to_frame(target, rows_there, tok_all.at[c, me], tok_send, tok_recv.at[c]).start()

    def send_rest():
        send_tokens(range(1, chunks))

    def start_sends():
        with jax.named_scope("w_barrier"):
            pl.semaphore_wait(barrier, frames)
        to_partner(tok_h.at[0], partner_tok, partner_send, partner_recv.at[0]).start()
        to_partner(vis_h, partner_vis, vis_send, partner_recv.at[1]).start()
        for k in ring:
            target = lax.rem(me + k, frames)
            to_frame(target, vis_h, vis_all.at[me], vis_send, vis_recv).start()
        send_tokens(range(1))
        pl.when(band == 0)(send_rest)
        for c in range(chunks):
            start = pl.multiple_of(me * mine + c * part_rows, part_rows)
            pltpu.make_async_copy(
                tok_h.at[0, pl.ds(start, part_rows)], tok_all.at[c, me], tok_recv.at[c]
            ).start()
        pltpu.make_async_copy(vis_h, vis_all.at[me], vis_recv).start()
        to_partner(gst_h.at[0, edge_row], halos.at[0], halo_send, halo_recv.at[0]).start()

    slot = jnp.where(me == 0, 2, jnp.where(me <= frames // 4, 1, 0))

    def at_slot(n):
        pl.when(slot == n)(start_sends)

    at_slot(0)
    with jax.named_scope("w_loads"):
        loaded(0)
    def share_edge(stage, value):
        stages[stage - 1, :, :] = value
        to_partner(
            stages.at[stage - 1, pl.ds(edge, columns)],
            halos.at[stage],
            halo_send,
            halo_recv.at[stage],
        ).start()

    def edge_here(stage):
        pltpu.make_async_copy(halos.at[stage], halos.at[stage], halo_recv.at[stage]).wait()

    def add_halo(acc, stage, w_ref, low):
        taps = column_taps(halos[stage].astype(F32), columns)
        weight = w_ref[pl.ds((1 - band) * 2, 1), :, low : low + GRU_WIDTH, :]
        weight = weight.reshape(3 * GRU_WIDTH, weight.shape[3])
        acc[pl.ds(edge, columns), :] += dot(taps, weight)

    def gates_of_state(state, stage):
        acc_g[...] = interior_conv(state, wg, 0, columns)
        edge_here(stage)
        add_halo(acc_g, stage, wg, 0)

    def reset_of(state, stage):
        acc_g[...] += ctx_g[...]
        reset = jax.nn.sigmoid(acc_g[:, GRU_WIDTH:])
        reset_state = (reset * state).astype(BF16)
        share_edge(stage, reset_state)
        acc_c[...] = ctx_c[...] + interior_conv(reset_state.astype(F32), wc, 0, columns)

    def state_after(state, stage):
        update = jax.nn.sigmoid(acc_g[:, :GRU_WIDTH])
        with jax.named_scope("w_hr%d" % stage):
            edge_here(stage)
        add_halo(acc_c, stage, wc, 0)
        candidate = jnp.tanh(acc_c[...])
        return ((1.0 - update) * state + update * candidate).astype(BF16)

    lane_head = lax.div(iota((1, channels), 1), HEAD_DIM)
    attended[...] = jnp.zeros_like(attended)
    tops[...] = jnp.zeros_like(tops)
    totals[...] = jnp.zeros_like(totals)

    def attend_half(half, track_rows, seen):
        keys[...] = dot(track_rows, wpk[...]).astype(BF16)
        values[...] = dot(track_rows, wpv[...]).astype(BF16)
        bias = jnp.where(seen > 0, 0.0, MASKED)

        def pixel_head(h, carry):
            chosen = jnp.where(lane_head == h, 1.0, 0.0)
            scores = dot_nt(queries[...] * chosen.astype(BF16), keys[...])
            scores = scores * LOGIT_SCALE + bias
            top = jnp.max(scores, axis=-1, keepdims=True)
            powers = jnp.exp2(scores - top)
            total = jnp.sum(powers, axis=-1, keepdims=True)
            tops[half] += top * chosen
            totals[half] += total * chosen
            attended[half] += dot(powers.astype(BF16), values[...]) * chosen
            return carry

        if half == 0:
            lax.fori_loop(0, HEADS // 2, pixel_head, 0, unroll=UNROLL)
            at_slot(1)
            lax.fori_loop(HEADS // 2, HEADS, pixel_head, 0, unroll=UNROLL)
            at_slot(2)
        else:
            lax.fori_loop(0, HEADS // 2, pixel_head, 0, unroll=UNROLL)
            pl.when(band > 0)(send_rest)
            lax.fori_loop(HEADS // 2, HEADS, pixel_head, 0, unroll=UNROLL)

    loaded(1)
    loaded(2)
    queries[...] = dot(pix[0].reshape(pixels, channels), wpq[...]).astype(BF16)

    with jax.named_scope("s_half0"):
        attend_half(0, tok[0], vis[...])
    for n in (5, 6, 7):
        loaded(n)
    state = gst[0].reshape(pixels, GRU_WIDTH).astype(F32)
    with jax.named_scope("s_g0"):
        gates_of_state(state, 0)
    with jax.named_scope("w_partner"):
        to_partner(tok_h.at[0], partner_tok, partner_send, partner_recv.at[0]).wait_recv()
        to_partner(vis_h, partner_vis, vis_send, partner_recv.at[1]).wait_recv()
    with jax.named_scope("s_half1"):
        attend_half(1, partner_tok[...], partner_vis[...])
    highest = jnp.maximum(tops[0], tops[1])
    share_0 = jnp.exp2(tops[0] - highest)
    share_1 = jnp.exp2(tops[1] - highest)
    merged = (attended[0] * share_0 + attended[1] * share_1) / (
        totals[0] * share_0 + totals[1] * share_1
    )
    loaded(3)
    context = dot(merged.astype(BF16), wpo[...]).astype(BF16)

    share_edge(1, context)


    loaded(4)
    with jax.named_scope("w_vis"):
        pltpu.make_async_copy(vis_all, vis_all, vis_recv).wait()

    blocks = mine // TILE
    key_rows = HEADS * TILE
    pair = LANES // key_rows
    first_mine = me * mine
    picked = iota((tracks, mine), 0) == first_mine + iota((tracks, mine), 1)
    picked = jnp.where(picked, 1.0, 0.0).astype(BF16)
    seen_rows = vis_all[...].reshape(frames, tracks).astype(F32).astype(BF16)
    seen_mine = dot(seen_rows, picked).astype(BF16)
    spread_shape = (mine, blocks * LANES)
    slot = iota(spread_shape, 1)
    spread = iota(spread_shape, 0) == lax.div(slot, LANES) * TILE + lax.rem(slot, TILE)
    spread = jnp.where(spread, 1.0, 0.0).astype(BF16)
    hidden = (dot(seen_mine, spread) - 1.0) * -MASKED
    lane_slot = lax.div(iota((1, LANES), 1), key_rows)
    for g in range(0, frames, pair):
        row = hidden[g : g + 1]
        for k in range(1, pair):
            chosen = lax.rem(lax.div(iota(row.shape, 1), key_rows), pair) == k
            row = jnp.where(chosen, hidden[g + k : g + k + 1], row)
        seen_bias[g // pair : g // pair + 1, :] = row
    picked_rows = iota((mine, tracks), 1) == first_mine + iota((mine, tracks), 0)
    picked_rows = jnp.where(picked_rows, 1.0, 0.0).astype(BF16)
    query_rows = jnp.broadcast_to(qfr[...].astype(F32), (LANES, tracks)).astype(BF16)
    query_col = dot_nt(picked_rows, query_rows)
    same_track = iota((TILE, LANES), 0) == lax.rem(iota((TILE, LANES), 1), TILE)
    heads_half = LANES // HEAD_DIM
    head_masks = []
    for first in range(0, heads_half, 2):
        wanted = first + lax.div(iota((2 * TILE, LANES), 0), TILE)
        head_masks.append(
            jnp.where(lax.div(iota((2 * TILE, LANES), 1), HEAD_DIM) == wanted, 1.0, 0.0).astype(BF16)
        )
    empty = jnp.zeros((2 * TILE, LANES), BF16)
    halves = channels // LANES
    group = 2 * pair

    def by_head(values_32):
        doubled = jnp.concatenate([values_32, values_32], axis=0).astype(BF16)
        out = []
        for half in range(halves):
            part = doubled[:, half * LANES : (half + 1) * LANES]
            for mask in head_masks:
                pieces = [empty] * halves
                pieces[half] = part * mask
                out.append(jnp.concatenate(pieces, axis=1))
        return out

    late = range(frames // 4, frames // 2)
    back_order = [[] for _ in range(chunks)]
    for c in range(chunks - 1):
        back_order[c] = [(c, n) for n in range(frames - 1) if n not in late]
    back_order[-1] = [(chunks - 1, 0)]
    back_order[-1] += [(chunks - 1, n) for n in range(frames // 2, frames - 1)]
    back_later = [(chunks - 1, n) for n in range(1, frames // 4)]
    back_later += [(c, n) for c in range(chunks - 1) for n in range(frames - 1) if n in late]
    back_later += [(chunks - 1, n) for n in range(frames // 4, frames // 2)]

    def send_back(pieces):
        for part, n in pieces:
            target = n + lax.div(n + frames - me, frames)
            to_frame(
                target,
                att_out.at[part, target],
                returned.at[part, me],
                back_send,
                back_recv.at[part],
            ).start()

    def attend_time(c):
        with jax.named_scope("w_tok%d" % c):
            pltpu.make_async_copy(tok_all.at[c], tok_all.at[c], tok_recv.at[c]).wait()
        flat = tok_all[c].reshape(frames * part_rows, channels)
        t_q = dot(flat, wtq[...]).astype(BF16).astype(F32)
        t_k = dot(flat, wtk[...])
        t_v = halves_dot(flat, wtv[...])
        tiles = range(part_rows // TILE)
        products = []
        for tile in tiles:

            def frame_rows(x, f):
                return x[f * part_rows + tile * TILE : f * part_rows + (tile + 1) * TILE]

            block = c * len(tiles) + tile
            asked = query_col[block * TILE : (block + 1) * TILE]
            asked = jnp.concatenate([asked] * halves, axis=1)
            q_frames = [frame_rows(t_q, f) for f in range(frames)]
            anchor = q_frames[0]
            for f in range(1, frames):
                anchor = jnp.where(asked == f, q_frames[f], anchor)
            joint = jnp.concatenate([q + anchor for q in q_frames], axis=0).astype(BF16)
            for g in range(0, frames, group):
                tile_keys = sum([by_head(frame_rows(t_k, g + k)) for k in range(group)], [])
                products.append(dot_nt(joint, jnp.concatenate(tile_keys, axis=0)))
        weights = []
        groups_of = frames // group
        for tile in tiles:
            block = c * len(tiles) + tile
            scores = []
            for n in range(frames // pair):
                product = products[tile * groups_of + n * pair // group]
                first = n * pair % group // pair * LANES
                bias = seen_bias[n : n + 1, block * LANES : (block + 1) * LANES]
                scores.append(product[:, first : first + LANES] * LOGIT_SCALE + bias)
            top = scores[0]
            for s in scores[1:]:
                top = jnp.maximum(top, s)
            turned = top
            for k in range(1, pair):
                top = jnp.maximum(top, pltpu.roll(turned, k * key_rows, 1))
            powers = [jnp.exp2(s - top) for s in scores]
            total = powers[0]
            for p in powers[1:]:
                total = total + p
            turned = total
            for k in range(1, pair):
                total = total + pltpu.roll(turned, k * key_rows, 1)
            keep = jnp.concatenate([same_track] * frames, axis=0)
            inverse = jnp.where(keep, 1.0 / total, 0.0)
            weights.append([(p * inverse).astype(BF16) for p in powers])
        results = []
        for tile in tiles:

            def frame_rows(x, f):
                return x[f * part_rows + tile * TILE : f * part_rows + (tile + 1) * TILE]

            tile_values = sum([by_head(frame_rows(t_v, f)) for f in range(frames)], [])
            results.append(
                dot(
                    jnp.concatenate(weights[tile], axis=1), jnp.concatenate(tile_values, axis=0)
                )
            )
        for f in range(frames):
            att_out[c, f] = jnp.concatenate(
                [r[f * TILE : (f + 1) * TILE] for r in results], axis=0
            ).astype(BF16)
        pltpu.make_async_copy(att_out.at[c, me], returned.at[c, me], back_recv.at[c]).start()
        send_back(back_order[c])

    for c in range(chunks):
        with jax.named_scope("s_time%d" % c):
            attend_time(c)
    context_f32 = context.astype(F32)
    with jax.named_scope("s_gctx"):
        ctx_g[...] = interior_conv(context_f32, wg, GRU_WIDTH, columns)
        ctx_c[...] = interior_conv(context_f32, wc, GRU_WIDTH, columns)
    pl.when(band == 0)(lambda: send_back(back_later))
    with jax.named_scope("w_hctx"):
        edge_here(1)
    add_halo(ctx_g, 1, wg, GRU_WIDTH)
    add_halo(ctx_c, 1, wc, GRU_WIDTH)
    with jax.named_scope("s_reset1"):
        reset_of(state, 2)
    pl.when(band > 0)(lambda: send_back(back_later))
    with jax.named_scope("s_state1"):
        new_state = state_after(state, 2)
    share_edge(3, new_state)

    for iteration in range(1, ITERS):
        state = new_state.astype(F32)
        with jax.named_scope("s_g1"):
            gates_of_state(state, 1 + 2 * iteration)
            reset_of(state, 2 + 2 * iteration)
        with jax.named_scope("s_state2"):
            new_state = state_after(state, 2 + 2 * iteration)
        if iteration < ITERS - 1:
            share_edge(3 + 2 * iteration, new_state)
    state_new[...] = new_state.reshape(1, rows, columns, GRU_WIDTH)
    out_copies = [pltpu.make_async_copy(state_new, out_state, out_sem.at[0])]
    out_copies[0].start()

    for c in range(chunks):
        with jax.named_scope("w_back%d" % c):
            pltpu.make_async_copy(returned.at[c], returned.at[c], back_recv.at[c]).wait()
        with jax.named_scope("s_final%d" % c):
            update = halves_dot(returned[c].reshape(frames * part_rows, channels), wto[...])
            for owner in range(frames):
                there = slice(owner * mine + c * part_rows, owner * mine + (c + 1) * part_rows)
                change = update[owner * part_rows : (owner + 1) * part_rows]
                track_new[0, there] = (tok[0, there].astype(F32) + change).astype(BF16)
    out_copies.append(pltpu.make_async_copy(track_new, out_track, out_sem.at[1]))
    out_copies[1].start()
    with jax.named_scope("w_out"):
        for copy in out_copies:
            copy.wait()
    with jax.named_scope("w_send"):
        sent = tok_all.at[:, 0 : frames - 1]
        to_partner(tok_h.at[0], partner_tok, partner_send, partner_recv.at[0]).wait_send()
        pltpu.make_async_copy(vis_all, vis_all, vis_send).wait()
        pltpu.make_async_copy(sent, sent, tok_send).wait()
        pltpu.make_async_copy(sent, sent, back_send).wait()
        pltpu.make_async_copy(halos, halos, halo_send).wait()


def deliver(state, track, out_state, out_track, sems):
    copies = [
        pltpu.make_async_copy(track, out_track, sems.at[0]),
        pltpu.make_async_copy(state, out_state, sems.at[1]),
    ]
    for copy in copies:
        copy.start()
    for copy in copies:
        copy.wait()


def on_device(frames, bands, *args):
    args = list(args)
    args[4] = args[4].reshape(1, -1)
    pixels, gru_state, tokens, visible = args[:4]
    tracks, channels = tokens.shape[1:]
    mine = tracks // frames
    chunks = CHUNKS if mine % (2 * CHUNKS * TILE) == 0 else 1
    part_rows = mine // chunks
    rows, columns = pixels.shape[1:3]
    count = rows * columns
    halo_stages = 1 + 2 * ITERS
    pair = LANES // (HEADS * TILE)
    dma = pltpu.SemaphoreType.DMA
    scratch = [
        pltpu.VMEM((7, channels, channels), BF16),
        pltpu.VMEM(pixels.shape, BF16),
        pltpu.VMEM(gru_state.shape, BF16),
        pltpu.VMEM(tokens.shape, BF16),
        pltpu.VMEM((2, tracks), jnp.int32),
        pltpu.VMEM(args[8].shape, BF16),
        pltpu.VMEM(args[13].shape, BF16),
        pltpu.VMEM(args[14].shape, BF16),
        pltpu.VMEM((tracks, channels), BF16),
        pltpu.VMEM((1, tracks), jnp.int32),
        pltpu.VMEM((chunks, frames, part_rows, channels), BF16),
        pltpu.VMEM((frames, 1, tracks), jnp.int32),
        pltpu.VMEM((count, channels), BF16),
        pltpu.VMEM((tracks, channels), BF16),
        pltpu.VMEM((tracks, channels), BF16),
        pltpu.VMEM((chunks, frames, part_rows, channels), BF16),
        pltpu.VMEM((chunks, frames, part_rows, channels), BF16),
        pltpu.VMEM((frames // pair, mine // TILE * LANES), F32),
        pltpu.VMEM((halo_stages - 1, count, GRU_WIDTH), BF16),
        pltpu.VMEM((halo_stages, columns, GRU_WIDTH), BF16),
        pltpu.VMEM((2, count, channels), F32),
        pltpu.VMEM((2, count, channels), F32),
        pltpu.VMEM((2, count, channels), F32),
        pltpu.VMEM((count, 2 * GRU_WIDTH), F32),
        pltpu.VMEM((count, GRU_WIDTH), F32),
        pltpu.VMEM((count, 2 * GRU_WIDTH), F32),
        pltpu.VMEM((count, GRU_WIDTH), F32),
        pltpu.VMEM(gru_state.shape, BF16),
        pltpu.VMEM(tokens.shape, BF16),
        dma((8,)),
        dma,
        dma((2,)),
        dma,
        dma((chunks,)),
        dma,
        dma,
        dma,
        dma((chunks,)),
        dma,
        dma((halo_stages,)),
        dma((2,)),
    ]

    def body(*refs):
        kernel(frames, bands, *refs)

    state, track = pl.pallas_call(
        body,
        out_shape=(
            pltpu.VMEM(gru_state.shape, BF16),
            pltpu.VMEM(tokens.shape, BF16),
        ),
        in_specs=[pl.BlockSpec(memory_space=pl.ANY)] * N_IN,
        out_specs=(pl.BlockSpec(memory_space=pl.ANY),) * 2,
        scratch_shapes=scratch,
        compiler_params=pltpu.CompilerParams(collective_id=0, has_side_effects=True),
        name="track_step",
    )(*args)
    return pl.pallas_call(
        deliver,
        out_shape=(
            jax.ShapeDtypeStruct(gru_state.shape, BF16),
            jax.ShapeDtypeStruct(tokens.shape, BF16),
        ),
        in_specs=[pl.BlockSpec(memory_space=pltpu.VMEM)] * 2,
        out_specs=(pl.BlockSpec(memory_space=pl.ANY),) * 2,
        scratch_shapes=[dma((2,))],
        name="track_deliver",
    )(pltpu.with_memory_space_constraint(state, pltpu.VMEM), pltpu.with_memory_space_constraint(track, pltpu.VMEM))


def solution(mesh):
    frames, bands = mesh.shape["frame"], mesh.shape["band"]
    placed = (
        P(("clip", "frame"), "band", None, None),
        P(("clip", "frame"), "band", None, None),
        P(("clip", "frame"), "band", None),
        P(("clip", "frame"), "band"),
        P(("clip", "band")),
    ) + (P(),) * 10
    return jax.shard_map(
        lambda *args: on_device(frames, bands, *args),
        mesh=mesh,
        in_specs=placed,
        out_specs=(P(("clip", "frame"), "band", None, None), P(("clip", "frame"), "band", None)),
        check_vma=False,
    )
```

```python
import math

import jax
import jax.numpy as jnp
from jax import lax
from jax.experimental import pallas as pl
from jax.experimental.pallas import tpu as pltpu
from jax.sharding import PartitionSpec as P

HEADS = 8
HEAD_DIM = 32
GRU_WIDTH = 128
ITERS = 2
LOGIT_SCALE = HEAD_DIM ** (-0.5) * math.log2(math.e)
MASKED = -1e30
TILE = 8
LANES = 128
MESH = pl.DeviceIdType.MESH
F32 = jnp.float32
BF16 = jnp.bfloat16
N_IN = 15
UNROLL = 4
CHUNKS = 2


def dot(a, b):
    return jnp.dot(a, b, preferred_element_type=F32)


def halves_dot(a, b):
    half = a.shape[0] // 2
    return jnp.concatenate([dot(a[:half], b), dot(a[half:], b)], axis=0)


def dot_nt(a, b):
    return lax.dot_general(a, b, (((1,), (1,)), ((), ())), preferred_element_type=F32)


def iota(shape, dim):
    return lax.broadcasted_iota(jnp.int32, shape, dim)


def column_taps(x, columns):
    length = x.shape[0]
    col = lax.rem(iota(x.shape, 0), columns)
    left = jnp.where(col == 0, 0.0, pltpu.roll(x, 1, 0))
    right = jnp.where(col == columns - 1, 0.0, pltpu.roll(x, length - 1, 0))
    return jnp.concatenate([left.astype(BF16), x.astype(BF16), right.astype(BF16)], axis=1)


def interior_conv(x, w_ref, low, columns):
    width = x.shape[1]
    taps = column_taps(x, columns)
    zero = jnp.zeros((columns, taps.shape[1]), BF16)
    above = jnp.concatenate([zero, taps[:-columns]], axis=0)
    below = jnp.concatenate([taps[columns:], zero], axis=0)
    patches = jnp.concatenate([above, taps, below], axis=1)
    weight = w_ref[:, :, low : low + width, :]
    return dot(patches, weight.reshape(9 * width, weight.shape[3]))


def kernel(frames, bands, *refs):
    inputs, refs = refs[:N_IN], refs[N_IN:]
    (out_state, out_track), refs = refs[:2], refs[2:]
    (
        squares,
        pix,
        gst,
        tok,
        ints,
        wpo,
        wg,
        wc,
        partner_tok,
        partner_vis,
        tok_all,
        vis_all,
        queries,
        keys,
        values,
        att_out,
        returned,
        seen_bias,
        stages,
        halos,
        attended,
        tops,
        totals,
        acc_g,
        acc_c,
        ctx_g,
        ctx_c,
        state_new,
        track_new,
        load_sem,
        partner_send,
        partner_recv,
        tok_send,
        tok_recv,
        vis_send,
        vis_recv,
        back_send,
        back_recv,
        halo_send,
        halo_recv,
        out_sem,
    ) = refs
    (pix_h, gst_h, tok_h, vis_h, qfr_h) = inputs[:5]
    (wpq_h, wpk_h, wpv_h, wpo_h, wtq_h, wtk_h, wtv_h, wto_h, wg_h, wc_h) = inputs[5:]
    wpk, wpv, wpq, wtq, wtk, wtv, wto = [squares.at[i] for i in range(7)]
    vis, qfr = ints.at[0:1], ints.at[1:2]
    me = lax.axis_index("frame")
    band = lax.axis_index("band")
    other = lax.rem(band + 1, bands)
    tracks, channels = tok.shape[1], tok.shape[2]
    mine = tracks // frames
    chunks, part_rows = tok_all.shape[0], tok_all.shape[2]
    rows, columns = pix.shape[1], pix.shape[2]
    pixels = rows * columns

    barrier = pltpu.get_barrier_semaphore()
    for k in range(1, frames):
        pl.semaphore_signal(
            barrier, inc=1, device_id={"frame": lax.rem(me + k, frames)}, device_id_type=MESH
        )
    pl.semaphore_signal(barrier, inc=1, device_id={"band": other}, device_id_type=MESH)

    groups = (
        ((tok_h, tok), (wpk_h, wpk), (wpv_h, wpv)),
        ((pix_h, pix), (wpq_h, wpq)),
        ((vis_h, vis), (qfr_h, qfr)),
        ((wpo_h, wpo),),
        ((wtq_h, wtq), (wtk_h, wtk), (wtv_h, wtv), (wto_h, wto)),
        ((gst_h, gst),),
        ((wg_h, wg),),
        ((wc_h, wc),),
    )
    whole = (squares.at[0:4], squares.at[0:2], ints, wpo, squares.at[0:4], gst, wg, wc)
    for n, group in enumerate(groups):
        for src, dst in group:
            pltpu.make_async_copy(src, dst, load_sem.at[n]).start()

    def loaded(n):
        pltpu.make_async_copy(whole[n], whole[n], load_sem.at[n]).wait()

    def to_partner(src, dst, send, recv):
        return pltpu.make_async_remote_copy(
            src_ref=src,
            dst_ref=dst,
            send_sem=send,
            recv_sem=recv,
            device_id={"band": other},
            device_id_type=MESH,
        )

    def to_frame(target, src, dst, send, recv):
        return pltpu.make_async_remote_copy(
            src_ref=src,
            dst_ref=dst,
            send_sem=send,
            recv_sem=recv,
            device_id={"frame": target},
            device_id_type=MESH,
        )

    edge_row = (1 - band) * (rows - 1)
    edge = pl.multiple_of(edge_row * columns, columns)
    ring = sorted(range(1, frames), key=lambda k: -min(k, frames - k))

    def send_tokens(parts):
        for c in parts:
            for k in ring:
                target = lax.rem(me + k, frames)
                start = pl.multiple_of(target * mine + c * part_rows, part_rows)
                rows_there = tok_h.at[0, pl.ds(start, part_rows)]
                to_frame(target, rows_there, tok_all.at[c, me], tok_send, tok_recv.at[c]).start()

    def send_rest():
        send_tokens(range(1, chunks))

    def start_sends():
        with jax.named_scope("w_barrier"):
            pl.semaphore_wait(barrier, frames)
        to_partner(tok_h.at[0], partner_tok, partner_send, partner_recv.at[0]).start()
        to_partner(vis_h, partner_vis, vis_send, partner_recv.at[1]).start()
        for k in ring:
            target = lax.rem(me + k, frames)
            to_frame(target, vis_h, vis_all.at[me], vis_send, vis_recv).start()
        send_tokens(range(1))
        pl.when(band == 0)(send_rest)
        for c in range(chunks):
            start = pl.multiple_of(me * mine + c * part_rows, part_rows)
            pltpu.make_async_copy(
                tok_h.at[0, pl.ds(start, part_rows)], tok_all.at[c, me], tok_recv.at[c]
            ).start()
        pltpu.make_async_copy(vis_h, vis_all.at[me], vis_recv).start()
        to_partner(gst_h.at[0, edge_row], halos.at[0], halo_send, halo_recv.at[0]).start()

    slot = jnp.where(me == 0, 2, jnp.where(me <= frames // 4, 1, 0))

    def at_slot(n):
        pl.when(slot == n)(start_sends)

    at_slot(0)
    with jax.named_scope("w_loads"):
        loaded(0)
    def share_edge(stage, value):
        stages[stage - 1, :, :] = value
        to_partner(
            stages.at[stage - 1, pl.ds(edge, columns)],
            halos.at[stage],
            halo_send,
            halo_recv.at[stage],
        ).start()

    def edge_here(stage):
        pltpu.make_async_copy(halos.at[stage], halos.at[stage], halo_recv.at[stage]).wait()

    def add_halo(acc, stage, w_ref, low):
        taps = column_taps(halos[stage].astype(F32), columns)
        weight = w_ref[pl.ds((1 - band) * 2, 1), :, low : low + GRU_WIDTH, :]
        weight = weight.reshape(3 * GRU_WIDTH, weight.shape[3])
        acc[pl.ds(edge, columns), :] += dot(taps, weight)

    def gates_of_state(state, stage):
        acc_g[...] = interior_conv(state, wg, 0, columns)
        edge_here(stage)
        add_halo(acc_g, stage, wg, 0)

    def reset_of(state, stage):
        acc_g[...] += ctx_g[...]
        reset = jax.nn.sigmoid(acc_g[:, GRU_WIDTH:])
        reset_state = (reset * state).astype(BF16)
        share_edge(stage, reset_state)
        acc_c[...] = ctx_c[...] + interior_conv(reset_state.astype(F32), wc, 0, columns)

    def state_after(state, stage):
        update = jax.nn.sigmoid(acc_g[:, :GRU_WIDTH])
        with jax.named_scope("w_hr%d" % stage):
            edge_here(stage)
        add_halo(acc_c, stage, wc, 0)
        candidate = jnp.tanh(acc_c[...])
        return ((1.0 - update) * state + update * candidate).astype(BF16)

    lane_head = lax.div(iota((1, channels), 1), HEAD_DIM)
    attended[...] = jnp.zeros_like(attended)
    tops[...] = jnp.zeros_like(tops)
    totals[...] = jnp.zeros_like(totals)

    def attend_half(half, track_rows, seen):
        keys[...] = dot(track_rows, wpk[...]).astype(BF16)
        values[...] = dot(track_rows, wpv[...]).astype(BF16)
        bias = jnp.where(seen > 0, 0.0, MASKED)

        def pixel_head(h, carry):
            chosen = jnp.where(lane_head == h, 1.0, 0.0)
            scores = dot_nt(queries[...] * chosen.astype(BF16), keys[...])
            scores = scores * LOGIT_SCALE + bias
            top = jnp.max(scores, axis=-1, keepdims=True)
            powers = jnp.exp2(scores - top)
            total = jnp.sum(powers, axis=-1, keepdims=True)
            tops[half] += top * chosen
            totals[half] += total * chosen
            attended[half] += dot(powers.astype(BF16), values[...]) * chosen
            return carry

        if half == 0:
            lax.fori_loop(0, HEADS // 2, pixel_head, 0, unroll=UNROLL)
            at_slot(1)
            lax.fori_loop(HEADS // 2, HEADS, pixel_head, 0, unroll=UNROLL)
            at_slot(2)
        else:
            lax.fori_loop(0, HEADS // 2, pixel_head, 0, unroll=UNROLL)
            pl.when(band > 0)(send_rest)
            lax.fori_loop(HEADS // 2, HEADS, pixel_head, 0, unroll=UNROLL)

    loaded(1)
    loaded(2)
    queries[...] = dot(pix[0].reshape(pixels, channels), wpq[...]).astype(BF16)

    with jax.named_scope("s_half0"):
        attend_half(0, tok[0], vis[...])
    for n in (5, 6, 7):
        loaded(n)
    state = gst[0].reshape(pixels, GRU_WIDTH).astype(F32)
    with jax.named_scope("s_g0"):
        gates_of_state(state, 0)
    with jax.named_scope("w_partner"):
        to_partner(tok_h.at[0], partner_tok, partner_send, partner_recv.at[0]).wait_recv()
        to_partner(vis_h, partner_vis, vis_send, partner_recv.at[1]).wait_recv()
    with jax.named_scope("s_half1"):
        attend_half(1, partner_tok[...], partner_vis[...])
    highest = jnp.maximum(tops[0], tops[1])
    share_0 = jnp.exp2(tops[0] - highest)
    share_1 = jnp.exp2(tops[1] - highest)
    merged = (attended[0] * share_0 + attended[1] * share_1) / (
        totals[0] * share_0 + totals[1] * share_1
    )
    loaded(3)
    context = dot(merged.astype(BF16), wpo[...]).astype(BF16)

    share_edge(1, context)


    loaded(4)
    with jax.named_scope("w_vis"):
        pltpu.make_async_copy(vis_all, vis_all, vis_recv).wait()

    blocks = mine // TILE
    key_rows = HEADS * TILE
    pair = LANES // key_rows
    first_mine = me * mine
    picked = iota((tracks, mine), 0) == first_mine + iota((tracks, mine), 1)
    picked = jnp.where(picked, 1.0, 0.0).astype(BF16)
    seen_rows = vis_all[...].reshape(frames, tracks).astype(F32).astype(BF16)
    seen_mine = dot(seen_rows, picked).astype(BF16)
    spread_shape = (mine, blocks * LANES)
    slot = iota(spread_shape, 1)
    spread = iota(spread_shape, 0) == lax.div(slot, LANES) * TILE + lax.rem(slot, TILE)
    spread = jnp.where(spread, 1.0, 0.0).astype(BF16)
    hidden = (dot(seen_mine, spread) - 1.0) * -MASKED
    lane_slot = lax.div(iota((1, LANES), 1), key_rows)
    for g in range(0, frames, pair):
        row = hidden[g : g + 1]
        for k in range(1, pair):
            chosen = lax.rem(lax.div(iota(row.shape, 1), key_rows), pair) == k
            row = jnp.where(chosen, hidden[g + k : g + k + 1], row)
        seen_bias[g // pair : g // pair + 1, :] = row
    picked_rows = iota((mine, tracks), 1) == first_mine + iota((mine, tracks), 0)
    picked_rows = jnp.where(picked_rows, 1.0, 0.0).astype(BF16)
    query_rows = jnp.broadcast_to(qfr[...].astype(F32), (LANES, tracks)).astype(BF16)
    query_col = dot_nt(picked_rows, query_rows)
    same_track = iota((TILE, LANES), 0) == lax.rem(iota((TILE, LANES), 1), TILE)
    heads_half = LANES // HEAD_DIM
    head_masks = []
    for first in range(0, heads_half, 2):
        wanted = first + lax.div(iota((2 * TILE, LANES), 0), TILE)
        head_masks.append(
            jnp.where(lax.div(iota((2 * TILE, LANES), 1), HEAD_DIM) == wanted, 1.0, 0.0).astype(BF16)
        )
    empty = jnp.zeros((2 * TILE, LANES), BF16)
    halves = channels // LANES
    group = 2 * pair

    def by_head(values_32):
        doubled = jnp.concatenate([values_32, values_32], axis=0).astype(BF16)
        out = []
        for half in range(halves):
            part = doubled[:, half * LANES : (half + 1) * LANES]
            for mask in head_masks:
                pieces = [empty] * halves
                pieces[half] = part * mask
                out.append(jnp.concatenate(pieces, axis=1))
        return out

    late = range(frames // 4, frames // 2)
    back_order = [[] for _ in range(chunks)]
    for c in range(chunks - 1):
        back_order[c] = [(c, n) for n in range(frames - 1) if n not in late]
    back_order[-1] = [(chunks - 1, 0)]
    back_order[-1] += [(chunks - 1, n) for n in range(frames // 2, frames - 1)]
    back_later = [(chunks - 1, n) for n in range(1, frames // 4)]
    back_later += [(c, n) for c in range(chunks - 1) for n in range(frames - 1) if n in late]
    back_later += [(chunks - 1, n) for n in range(frames // 4, frames // 2)]

    def send_back(pieces):
        for part, n in pieces:
            target = n + lax.div(n + frames - me, frames)
            to_frame(
                target,
                att_out.at[part, target],
                returned.at[part, me],
                back_send,
                back_recv.at[part],
            ).start()

    def attend_time(c):
        with jax.named_scope("w_tok%d" % c):
            pltpu.make_async_copy(tok_all.at[c], tok_all.at[c], tok_recv.at[c]).wait()
        flat = tok_all[c].reshape(frames * part_rows, channels)
        t_q = dot(flat, wtq[...]).astype(BF16).astype(F32)
        t_k = dot(flat, wtk[...])
        t_v = halves_dot(flat, wtv[...])
        tiles = range(part_rows // TILE)
        products = []
        for tile in tiles:

            def frame_rows(x, f):
                return x[f * part_rows + tile * TILE : f * part_rows + (tile + 1) * TILE]

            block = c * len(tiles) + tile
            asked = query_col[block * TILE : (block + 1) * TILE]
            asked = jnp.concatenate([asked] * halves, axis=1)
            q_frames = [frame_rows(t_q, f) for f in range(frames)]
            anchor = q_frames[0]
            for f in range(1, frames):
                anchor = jnp.where(asked == f, q_frames[f], anchor)
            joint = jnp.concatenate([q + anchor for q in q_frames], axis=0).astype(BF16)
            for g in range(0, frames, group):
                tile_keys = sum([by_head(frame_rows(t_k, g + k)) for k in range(group)], [])
                products.append(dot_nt(joint, jnp.concatenate(tile_keys, axis=0)))
        weights = []
        groups_of = frames // group
        for tile in tiles:
            block = c * len(tiles) + tile
            scores = []
            for n in range(frames // pair):
                product = products[tile * groups_of + n * pair // group]
                first = n * pair % group // pair * LANES
                bias = seen_bias[n : n + 1, block * LANES : (block + 1) * LANES]
                scores.append(product[:, first : first + LANES] * LOGIT_SCALE + bias)
            top = scores[0]
            for s in scores[1:]:
                top = jnp.maximum(top, s)
            turned = top
            for k in range(1, pair):
                top = jnp.maximum(top, pltpu.roll(turned, k * key_rows, 1))
            powers = [jnp.exp2(s - top) for s in scores]
            total = powers[0]
            for p in powers[1:]:
                total = total + p
            turned = total
            for k in range(1, pair):
                total = total + pltpu.roll(turned, k * key_rows, 1)
            keep = jnp.concatenate([same_track] * frames, axis=0)
            inverse = jnp.where(keep, 1.0 / total, 0.0)
            weights.append([(p * inverse).astype(BF16) for p in powers])
        results = []
        for tile in tiles:

            def frame_rows(x, f):
                return x[f * part_rows + tile * TILE : f * part_rows + (tile + 1) * TILE]

            tile_values = sum([by_head(frame_rows(t_v, f)) for f in range(frames)], [])
            results.append(
                dot(
                    jnp.concatenate(weights[tile], axis=1), jnp.concatenate(tile_values, axis=0)
                )
            )
        for f in range(frames):
            att_out[c, f] = jnp.concatenate(
                [r[f * TILE : (f + 1) * TILE] for r in results], axis=0
            ).astype(BF16)
        pltpu.make_async_copy(att_out.at[c, me], returned.at[c, me], back_recv.at[c]).start()
        send_back(back_order[c])

    for c in range(chunks):
        with jax.named_scope("s_time%d" % c):
            attend_time(c)
    context_f32 = context.astype(F32)
    with jax.named_scope("s_gctx"):
        ctx_g[...] = interior_conv(context_f32, wg, GRU_WIDTH, columns)
        ctx_c[...] = interior_conv(context_f32, wc, GRU_WIDTH, columns)
    pl.when(band == 0)(lambda: send_back(back_later))
    with jax.named_scope("w_hctx"):
        edge_here(1)
    add_halo(ctx_g, 1, wg, GRU_WIDTH)
    add_halo(ctx_c, 1, wc, GRU_WIDTH)
    with jax.named_scope("s_reset1"):
        reset_of(state, 2)
    pl.when(band > 0)(lambda: send_back(back_later))
    with jax.named_scope("s_state1"):
        new_state = state_after(state, 2)
    share_edge(3, new_state)

    for iteration in range(1, ITERS):
        state = new_state.astype(F32)
        with jax.named_scope("s_g1"):
            gates_of_state(state, 1 + 2 * iteration)
            reset_of(state, 2 + 2 * iteration)
        with jax.named_scope("s_state2"):
            new_state = state_after(state, 2 + 2 * iteration)
        if iteration < ITERS - 1:
            share_edge(3 + 2 * iteration, new_state)
    state_new[...] = new_state.reshape(1, rows, columns, GRU_WIDTH)
    out_copies = [pltpu.make_async_copy(state_new, out_state, out_sem.at[0])]
    out_copies[0].start()

    for c in range(chunks):
        with jax.named_scope("w_back%d" % c):
            pltpu.make_async_copy(returned.at[c], returned.at[c], back_recv.at[c]).wait()
        with jax.named_scope("s_final%d" % c):
            update = halves_dot(returned[c].reshape(frames * part_rows, channels), wto[...])
            for owner in range(frames):
                there = slice(owner * mine + c * part_rows, owner * mine + (c + 1) * part_rows)
                change = update[owner * part_rows : (owner + 1) * part_rows]
                track_new[0, there] = (tok[0, there].astype(F32) + change).astype(BF16)
    out_copies.append(pltpu.make_async_copy(track_new, out_track, out_sem.at[1]))
    out_copies[1].start()
    with jax.named_scope("w_out"):
        for copy in out_copies:
            copy.wait()
    with jax.named_scope("w_send"):
        sent = tok_all.at[:, 0 : frames - 1]
        to_partner(tok_h.at[0], partner_tok, partner_send, partner_recv.at[0]).wait_send()
        pltpu.make_async_copy(vis_all, vis_all, vis_send).wait()
        pltpu.make_async_copy(sent, sent, tok_send).wait()
        pltpu.make_async_copy(sent, sent, back_send).wait()
        pltpu.make_async_copy(halos, halos, halo_send).wait()


def deliver(state, track, out_state, out_track, sems):
    part = track.shape[1] // 4
    for n in range(4):
        there = pl.ds(n * part, part)
        pltpu.make_async_copy(track.at[0, there], out_track.at[0, there], sems.at[0]).start()
    pltpu.make_async_copy(state, out_state, sems.at[1]).start()
    pltpu.make_async_copy(track, out_track, sems.at[0]).wait()
    pltpu.make_async_copy(state, out_state, sems.at[1]).wait()


def on_device(frames, bands, *args):
    args = list(args)
    args[4] = args[4].reshape(1, -1)
    pixels, gru_state, tokens, visible = args[:4]
    tracks, channels = tokens.shape[1:]
    mine = tracks // frames
    chunks = CHUNKS if mine % (2 * CHUNKS * TILE) == 0 else 1
    part_rows = mine // chunks
    rows, columns = pixels.shape[1:3]
    count = rows * columns
    halo_stages = 1 + 2 * ITERS
    pair = LANES // (HEADS * TILE)
    dma = pltpu.SemaphoreType.DMA
    scratch = [
        pltpu.VMEM((7, channels, channels), BF16),
        pltpu.VMEM(pixels.shape, BF16),
        pltpu.VMEM(gru_state.shape, BF16),
        pltpu.VMEM(tokens.shape, BF16),
        pltpu.VMEM((2, tracks), jnp.int32),
        pltpu.VMEM(args[8].shape, BF16),
        pltpu.VMEM(args[13].shape, BF16),
        pltpu.VMEM(args[14].shape, BF16),
        pltpu.VMEM((tracks, channels), BF16),
        pltpu.VMEM((1, tracks), jnp.int32),
        pltpu.VMEM((chunks, frames, part_rows, channels), BF16),
        pltpu.VMEM((frames, 1, tracks), jnp.int32),
        pltpu.VMEM((count, channels), BF16),
        pltpu.VMEM((tracks, channels), BF16),
        pltpu.VMEM((tracks, channels), BF16),
        pltpu.VMEM((chunks, frames, part_rows, channels), BF16),
        pltpu.VMEM((chunks, frames, part_rows, channels), BF16),
        pltpu.VMEM((frames // pair, mine // TILE * LANES), F32),
        pltpu.VMEM((halo_stages - 1, count, GRU_WIDTH), BF16),
        pltpu.VMEM((halo_stages, columns, GRU_WIDTH), BF16),
        pltpu.VMEM((2, count, channels), F32),
        pltpu.VMEM((2, count, channels), F32),
        pltpu.VMEM((2, count, channels), F32),
        pltpu.VMEM((count, 2 * GRU_WIDTH), F32),
        pltpu.VMEM((count, GRU_WIDTH), F32),
        pltpu.VMEM((count, 2 * GRU_WIDTH), F32),
        pltpu.VMEM((count, GRU_WIDTH), F32),
        pltpu.VMEM(gru_state.shape, BF16),
        pltpu.VMEM(tokens.shape, BF16),
        dma((8,)),
        dma,
        dma((2,)),
        dma,
        dma((chunks,)),
        dma,
        dma,
        dma,
        dma((chunks,)),
        dma,
        dma((halo_stages,)),
        dma((2,)),
    ]

    def body(*refs):
        kernel(frames, bands, *refs)

    state, track = pl.pallas_call(
        body,
        out_shape=(
            pltpu.VMEM(gru_state.shape, BF16),
            pltpu.VMEM(tokens.shape, BF16),
        ),
        in_specs=[pl.BlockSpec(memory_space=pl.ANY)] * N_IN,
        out_specs=(pl.BlockSpec(memory_space=pl.ANY),) * 2,
        scratch_shapes=scratch,
        compiler_params=pltpu.CompilerParams(collective_id=0, has_side_effects=True),
        name="track_step",
    )(*args)
    return pl.pallas_call(
        deliver,
        out_shape=(
            jax.ShapeDtypeStruct(gru_state.shape, BF16),
            jax.ShapeDtypeStruct(tokens.shape, BF16),
        ),
        in_specs=[pl.BlockSpec(memory_space=pltpu.VMEM)] * 2,
        out_specs=(pl.BlockSpec(memory_space=pl.ANY),) * 2,
        scratch_shapes=[dma((2,))],
        name="track_deliver",
    )(pltpu.with_memory_space_constraint(state, pltpu.VMEM), pltpu.with_memory_space_constraint(track, pltpu.VMEM))


def solution(mesh):
    frames, bands = mesh.shape["frame"], mesh.shape["band"]
    placed = (
        P(("clip", "frame"), "band", None, None),
        P(("clip", "frame"), "band", None, None),
        P(("clip", "frame"), "band", None),
        P(("clip", "frame"), "band"),
        P(("clip", "band")),
    ) + (P(),) * 10
    return jax.shard_map(
        lambda *args: on_device(frames, bands, *args),
        mesh=mesh,
        in_specs=placed,
        out_specs=(P(("clip", "frame"), "band", None, None), P(("clip", "frame"), "band", None)),
        check_vma=False,
    )
```
